32 devices in a mesh: row: 8 (over y, x, core), col: 4 (over z).
Axes of the slice: x: 2, y: 2, z: 4, core: 2. Of those that a mesh axis runs over, the one named last changes fastest.
Arguments:
- image: bfloat16 [384, 256, 256], P('row', 'col'), may hold values from -6 to 6
- norm_gain: float32 [2, 2, 256], replicated, may hold values from 0.1 to 1.9
- conv_first: bfloat16 [2, 3, 3, 256, 256], replicated, may hold values from -0.125 to 0.125
- conv_second: bfloat16 [2, 3, 3, 256, 256], replicated, may hold values from -0.125 to 0.125
- proj_in: bfloat16 [2, 256, 512], replicated, may hold values from -0.375 to 0.375
- block_mix: bfloat16 [2, 256, 256], replicated, may hold values from -0.375 to 0.375
- block_bias: float32 [2, 256], replicated, may hold values from 0.5 to 1.5
- grid_mix: bfloat16 [2, 32, 32], replicated, may hold values from -1 to 1
- grid_bias: float32 [2, 32], replicated, may hold values from 0.5 to 1.5
- proj_out: bfloat16 [2, 256, 256], replicated, may hold values from -0.375 to 0.375
Outputs:
- restored: bfloat16 [384, 256, 256], P('row', 'col')
The draws below stay inside these ranges and needn't reach their ends.
All inputs are finite; a program needn't handle non-finite values.
Results may differ from the reference program's by a relative error of at most 0.012.
Values may be sent and summed in bfloat16 or wider, within the bound.
No kernel may reach another device: no remote copies, remote signals or barrier semaphores. Data moves between devices by JAX's collectives and lax.ppermute only.
A program may use at most 128 MiB of HBM per device.

```python
import jax
import jax.numpy as jnp
from jax import lax

C = 256
BLOCK = 16
LAYERS = 2
CH = 48
CW = 64
POSITIONS = 256
GRID = 32
NH = 384
NW = 256
N_ROW = 8
N_COL = 4


def block_scale(rng, shape, cuts, low, high):
    def one(dim, parts):
        draws = jax.random.uniform(jax.random.fold_in(jax.random.fold_in(rng, 6), dim), (parts,), jnp.float32, low / len(cuts), high / len(cuts))
        return jnp.repeat(jnp.exp(draws), shape[dim] // parts).reshape((-1,) + (1,) * (len(shape) - dim - 1))

    loudness = one(*cuts[0])
    for cut in cuts[1:]:
        loudness = loudness * one(*cut)
    return loudness


def scatter_about(own_key, dims, width, reach, split=(), held_as=jnp.bfloat16):
    result = jax.random.normal(own_key, dims, jnp.float32) * width
    if len(split) > 0:
        result = block_scale(own_key, dims, split, -0.22, 0.18) * result
    return jnp.clip(result, min=-reach, max=reach).astype(held_as)


def setup_inputs(seed: int = 0) -> dict:
    key_of = jax.random.split(jax.random.key(seed), 11)
    image = scatter_about(key_of[0], (NH, NW, C), 1.0, 6.0, ((0, 8), (1, 4)))
    norm_gain = jnp.clip(1.0 + 0.18 * jax.random.normal(key_of[1], (LAYERS, 2, C), jnp.float32), 0.1, 1.9)
    conv_first = scatter_about(key_of[2], (LAYERS, 3, 3, C, C), (9 * C) ** -0.5, 0.125)
    conv_second = scatter_about(key_of[3], (LAYERS, 3, 3, C, C), (9 * C) ** -0.5, 0.125)
    proj_in = scatter_about(key_of[4], (LAYERS, C, 2 * C), C ** -0.5, 0.375)
    block_mix = scatter_about(key_of[5], (LAYERS, POSITIONS, POSITIONS), POSITIONS ** -0.5, 0.375)
    block_bias = jnp.clip(jax.random.uniform(key_of[6], (LAYERS, POSITIONS), jnp.float32, 0.5, 1.5), 0.5, 1.5)
    grid_mix = scatter_about(key_of[7], (LAYERS, GRID, GRID), GRID ** -0.5, 1.0)
    grid_bias = jnp.clip(jax.random.uniform(key_of[8], (LAYERS, GRID), jnp.float32, 0.5, 1.5), 0.5, 1.5)
    proj_out = scatter_about(key_of[9], (LAYERS, C, C), C ** -0.5, 0.375)
    return {"image": image, "norm_gain": norm_gain, "conv_first": conv_first, "conv_second": conv_second, "proj_in": proj_in, "block_mix": block_mix, "block_bias": block_bias, "grid_mix": grid_mix, "grid_bias": grid_bias, "proj_out": proj_out}


epsilon = 1e-06

def layer_norm(field, gain_vector):
    values = field.astype(jnp.float32)
    average = lax.optimization_barrier(jnp.mean(values, axis=-1, keepdims=True))
    centred = values - average
    variance = lax.optimization_barrier(jnp.mean(centred * centred, axis=-1, keepdims=True))
    return centred * lax.rsqrt(variance + epsilon) * gain_vector

def convolve(padded, kernel, out_rows, out_cols):
    channels = padded.shape[-1]
    accumulated = jnp.zeros((out_rows * out_cols, kernel.shape[-1]), jnp.float32)
    for offset_row in range(3):
        for offset_col in range(3):
            window = padded[offset_row:offset_row + out_rows, offset_col:offset_col + out_cols].reshape(-1, channels)
            accumulated = accumulated + jnp.dot(window, kernel[offset_row, offset_col], preferred_element_type=jnp.float32)
    return accumulated.reshape(out_rows, out_cols, kernel.shape[-1])

def reference(image, norm_gain, conv_first, conv_second, proj_in, block_mix, block_bias, grid_mix, grid_bias, proj_out):
    height = CH * N_ROW
    breadth = CW * N_COL
    half_width = C // 2
    grid_cells = N_ROW * N_COL
    current = image
    for which_layer in range(LAYERS):
        normed = layer_norm(current, norm_gain[which_layer, 0]).astype(jnp.bfloat16)
        padded = jnp.pad(normed, ((1, 1), (1, 1), (0, 0)))
        first_conv = jax.nn.gelu(convolve(padded, conv_first[which_layer], height, breadth)).astype(jnp.bfloat16)
        padded_first = jnp.pad(first_conv, ((1, 1), (1, 1), (0, 0)))
        second_conv = convolve(padded_first, conv_second[which_layer], height, breadth)
        mixed_state = current.astype(jnp.float32) + second_conv
        normed_two = layer_norm(mixed_state, norm_gain[which_layer, 1]).astype(jnp.bfloat16).reshape(-1, C)
        expanded = jax.nn.gelu(jnp.dot(normed_two, proj_in[which_layer], preferred_element_type=jnp.float32)).astype(jnp.bfloat16)
        local_u = expanded[:, :half_width]
        local_v = expanded[:, half_width:C]
        global_u = expanded[:, C:C + half_width]
        global_v = expanded[:, C + half_width:]
        local_flat = local_v.reshape(height // BLOCK, BLOCK, breadth // BLOCK, BLOCK, half_width)
        local_flat = local_flat.transpose(1, 3, 0, 2, 4).reshape(BLOCK * BLOCK, -1)
        local_mixed = jnp.dot(block_mix[which_layer], local_flat, preferred_element_type=jnp.float32) + block_bias[which_layer][:, None]
        local_mixed = local_mixed.reshape(BLOCK, BLOCK, height // BLOCK, breadth // BLOCK, half_width)
        local_mixed = local_mixed.transpose(2, 0, 3, 1, 4).reshape(-1, half_width)
        gated_local = (local_u.astype(jnp.float32) * local_mixed).astype(jnp.bfloat16)
        global_flat = global_v.reshape(N_ROW, CH, N_COL, CW, half_width).transpose(0, 2, 1, 3, 4).reshape(grid_cells, -1)
        global_mixed = jnp.dot(grid_mix[which_layer], global_flat, preferred_element_type=jnp.float32) + grid_bias[which_layer][:, None]
        global_mixed = lax.optimization_barrier(global_mixed.astype(jnp.bfloat16))
        global_mixed = global_mixed.reshape(N_ROW, N_COL, CH, CW, half_width).transpose(0, 2, 1, 3, 4).reshape(-1, half_width)
        gated_global = (global_u.astype(jnp.float32) * global_mixed.astype(jnp.float32)).astype(jnp.bfloat16)
        joined = jnp.concatenate([gated_local, gated_global], axis=-1)
        projected = jnp.dot(joined, proj_out[which_layer], preferred_element_type=jnp.float32)
        current = (mixed_state + projected.reshape(height, breadth, C)).astype(jnp.bfloat16)
    return current
```

```python
import functools
import math

import jax
import jax.numpy as jnp
from jax import lax
from jax.experimental import pallas as pl
from jax.experimental.pallas import tpu as pltpu
from jax.sharding import PartitionSpec as P

BLOCK = 16
LAYERS = 2
RIM = 2
GROUP_ONE = 10
GROUP_TWO = 8
MIB = 1 << 20

epsilon = 1e-06
ROOT = math.sqrt(2.0 / math.pi)

VMEM = pl.BlockSpec(memory_space=pltpu.VMEM)
ANY = pl.BlockSpec(memory_space=pltpu.HBM)


def parity(axis):
    return lax.rem(lax.axis_index(axis), 2)


def edge_factors():
    factors = []
    for axis in ("row", "col"):
        place = lax.axis_index(axis)
        for end in (0, lax.axis_size(axis) - 1):
            factors.append(jnp.where(place == end, 0.0, 1.0))
    return factors


def gelu(v):
    return 0.5 * v * (1.0 + jnp.tanh(ROOT * (v + 0.044715 * (v * v * v))))


def normalised(values, gain_row):
    average = jnp.mean(values, axis=-1, keepdims=True)
    centred = values - average
    variance = jnp.mean(centred * centred, axis=-1, keepdims=True)
    return centred * lax.rsqrt(variance + epsilon) * gain_row


def rounded(values):
    return values.astype(jnp.bfloat16).astype(jnp.float32)


def largest_divisor(total, most):
    return max(d for d in range(1, most + 1) if total % d == 0)


def spread(row, left_row, right_row, dst_ref, i, cols):
    channels = row.shape[-1]
    place = lax.broadcasted_iota(jnp.int32, row.shape, 0)
    before = jnp.where(place == 0, left_row, pltpu.roll(row, 1, 0))
    after = jnp.where(place == cols - 1, right_row, pltpu.roll(row, cols - 1, 0))
    dst_ref[i, :, 0:channels] = before.astype(jnp.bfloat16)
    dst_ref[i, :, channels : 2 * channels] = row.astype(jnp.bfloat16)
    dst_ref[i, :, 2 * channels : 3 * channels] = after.astype(jnp.bfloat16)


def pipelined(count, multiply, finish, slots):
    multiply(0, slots[0])
    pairs = (count - 1) // 2

    @pl.loop(0, pairs)
    def _(k):
        for u in range(2):
            multiply(2 * k + u + 1, slots[(u + 1) % 2])
            finish(2 * k + u, slots[u])

    if count % 2 == 0:
        multiply(count - 1, slots[1])
        finish(count - 2, slots[0])
    finish(count - 1, slots[(count - 1) % 2])


def in_hbm(values):
    return pltpu.with_memory_space_constraint(values, pltpu.HBM)


def front_kernel(
    layer,
    cur_ref,
    near_rows,
    far_rows,
    near_cols,
    far_cols,
    gain_ref,
    first_hbm,
    second_hbm,
    in_proj_hbm,
    mixed_ref,
    lu_ref,
    lv_ref,
    gu_ref,
    gv_ref,
    one_ref,
    two_ref,
    sides_ref,
    left_side,
    right_side,
    left_one,
    right_one,
    slot_a,
    slot_b,
    slot_c,
    slot_d,
    first_ref,
    second_ref,
    in_ref,
    sems,
):
    rows, cols, channels = cur_ref.shape
    feed = [
        pltpu.make_async_copy(src.at[layer], dst, sems.at[k])
        for k, (src, dst) in enumerate(
            ((first_hbm, first_ref), (second_hbm, second_ref), (in_proj_hbm, in_ref))
        )
    ]
    for copy in feed:
        copy.start()
    half = channels // 2
    near_top = parity("row") == 1
    near_left = parity("col") == 1
    edge_ref = edge_factors()
    gain_one = gain_ref[layer, 0:1, :]
    gain_two = gain_ref[layer, 1:2, :]
    long = rows + 2 * RIM

    spot = lax.broadcasted_iota(jnp.int32, (long, channels), 0)
    within = jnp.where(spot < RIM, edge_ref[0], jnp.where(spot < long - RIM, 1.0, edge_ref[1]))

    def chosen(near_low, side, near, far):
        low, high = (near, far) if side == 0 else (far, near)
        return jnp.where(near_low, low.astype(jnp.float32), high.astype(jnp.float32))

    for side in range(2):
        for c in range(RIM):
            sides_ref[side * RIM + c, 0:long] = rounded(
                normalised(chosen(near_left, side, near_cols[c], far_cols[c]), gain_one)
            ) * (within * edge_ref[2 + side])
    left_side[0:long, 0:channels] = sides_ref[0, 0:long]
    left_side[0:long, channels : 2 * channels] = sides_ref[1, 0:long]
    right_side[0:long, channels : 2 * channels] = sides_ref[2, 0:long]
    right_side[0:long, 2 * channels : 3 * channels] = sides_ref[3, 0:long]

    def norm_row(values, dst, keep=None):
        row = rounded(normalised(values, gain_one))
        if keep is not None:
            row = row * keep
        spread(row, sides_ref[1, pl.ds(dst, 1)], sides_ref[2, pl.ds(dst, 1)], one_ref, dst, cols)
        left_side[pl.ds(dst, 1), 2 * channels : 3 * channels] = row[0:1]
        right_side[pl.ds(dst, 1), 0:channels] = row[cols - 1 : cols]

    for r in range(RIM):
        norm_row(chosen(near_top, 0, near_rows[r], far_rows[r]), r, edge_ref[0])
        norm_row(chosen(near_top, 1, near_rows[r], far_rows[r]), RIM + rows + r, edge_ref[1])

    unroll = largest_divisor(rows, 4)

    @pl.loop(0, rows // unroll)
    def _(step):
        for u in range(unroll):
            i = step * unroll + u
            norm_row(cur_ref[i].astype(jnp.float32), i + RIM)

    feed[0].wait()

    def windows(src_ref, base, count):
        return jnp.concatenate(
            [
                src_ref[pl.ds(base + a, count)].reshape(count * cols, 3 * channels)
                for a in range(3)
            ],
            axis=1,
        )

    tall = rows + 2
    padded = left_one.shape[0]
    place = lax.broadcasted_iota(jnp.int32, (padded, channels), 0)
    inside = jnp.where(place == 0, edge_ref[0], 1.0)
    inside = jnp.where(place == tall - 1, edge_ref[1], inside)
    group = slot_a.shape[0] // cols

    def first_multiply(g, slot):
        window = windows(one_ref, g * group, group)
        if isinstance(g, int) and g == 0:
            sides = [
                jnp.concatenate([side[a : a + padded] for a in range(3)], axis=1)
                for side in (left_side, right_side)
            ]
            window = jnp.concatenate([window] + [v.astype(jnp.bfloat16) for v in sides], axis=0)
        total = jnp.dot(window, first_ref[...], preferred_element_type=jnp.float32)
        slot[...] = total[: group * cols]
        if isinstance(g, int) and g == 0:
            for k, one_side in enumerate((left_one, right_one)):
                start = group * cols + k * padded
                one_side[...] = rounded(
                    gelu(total[start : start + padded]) * (inside * edge_ref[2 + k])
                )

    def first_finish(g, slot):
        for u in range(group):
            i = g * group + u
            keep = jnp.where(i == 0, edge_ref[0], jnp.where(i == tall - 1, edge_ref[1], 1.0))
            row = rounded(gelu(slot[u * cols : (u + 1) * cols])) * keep
            spread(row, left_one[pl.ds(i, 1)], right_one[pl.ds(i, 1)], two_ref, i, cols)

    pipelined(tall // group, first_multiply, first_finish, (slot_a, slot_b))

    feed[1].wait()
    feed[2].wait()
    many = slot_c.shape[0] // cols

    def second_multiply(g, slot):
        slot[...] = jnp.dot(
            windows(two_ref, g * many, many),
            second_ref[...],
            preferred_element_type=jnp.float32,
        )

    def second_finish(g, slot):
        where = pl.ds(pl.multiple_of(g * many * cols, many * cols), many * cols)
        total = slot[...] + cur_ref[pl.ds(g * many, many)].reshape(
            many * cols, channels
        ).astype(jnp.float32)
        mixed_ref[where] = total
        normed = normalised(total, gain_two).astype(jnp.bfloat16)
        expanded = gelu(
            jnp.dot(normed, in_ref[...], preferred_element_type=jnp.float32)
        ).astype(jnp.bfloat16)
        for k, out in enumerate((lu_ref, lv_ref, gu_ref, gv_ref)):
            out[where] = expanded[:, k * half : (k + 1) * half]

    pipelined(rows // many, second_multiply, second_finish, (slot_c, slot_d))

def front(layer, cur, rim_rows, rim_cols, gains, first, second, proj):
    rows, cols, channels = cur.shape
    pixels = rows * cols
    half = channels // 2
    long = rows + 2 * RIM
    padded = -(-(rows + 2) // 16) * 16
    tall = padded + 8
    group = largest_divisor(rows + 2, GROUP_ONE)
    many = largest_divisor(rows, GROUP_TWO)
    bf = jnp.bfloat16
    f32 = jnp.float32
    outs = [jax.ShapeDtypeStruct((pixels, channels), f32)]
    outs += [jax.ShapeDtypeStruct((pixels, half), bf)] * 4
    return pl.pallas_call(
        functools.partial(front_kernel, layer),
        out_shape=outs,
        in_specs=[VMEM] * 6 + [ANY] * 3,
        out_specs=[VMEM] * 5,
        scratch_shapes=[
            pltpu.VMEM((long, cols, 3 * channels), bf),
            pltpu.VMEM((rows + 2, cols, 3 * channels), bf),
            pltpu.VMEM((2 * RIM, tall, channels), f32),
            pltpu.VMEM((tall, 3 * channels), f32),
            pltpu.VMEM((tall, 3 * channels), f32),
            pltpu.VMEM((padded, channels), f32),
            pltpu.VMEM((padded, channels), f32),
            pltpu.VMEM((group * cols, channels), f32),
            pltpu.VMEM((group * cols, channels), f32),
            pltpu.VMEM((many * cols, channels), f32),
            pltpu.VMEM((many * cols, channels), f32),
            pltpu.VMEM(first.shape[1:], bf),
            pltpu.VMEM(second.shape[1:], bf),
            pltpu.VMEM(proj.shape[1:], bf),
            pltpu.SemaphoreType.DMA((3,)),
        ],
        compiler_params=pltpu.CompilerParams(vmem_limit_bytes=34 * MIB),
        cost_estimate=pl.CostEstimate(
            flops=2 * pixels * channels * channels * 20,
            bytes_accessed=12 << 20,
            transcendentals=3 * pixels * channels,
        ),
        name="front",
    )(cur, *rim_rows, *rim_cols, gains, *(in_hbm(w) for w in (first, second, proj)))


def local_kernel(
    layer, lu_ref, lv_ref, mix_ref, bias_ref, grid_ref, grid_bias_ref, out_ref, tiles_ref, shift_ref
):
    rows, cols, half = lu_ref.shape
    down, across = rows // BLOCK, cols // BLOCK
    pair = 2 if across % 2 == 0 else 1
    area = BLOCK * BLOCK
    spot = lax.broadcasted_iota(jnp.int32, (area, area), 0)
    same = spot == lax.broadcasted_iota(jnp.int32, (area, area), 1)
    bias = jnp.sum(jnp.where(same, bias_ref[layer : layer + 1], 0.0), axis=1, keepdims=True)
    for i in range(down):
        r = slice(i * BLOCK, (i + 1) * BLOCK)
        for j in range(0, across, pair):
            cut = [slice((j + k) * BLOCK, (j + k + 1) * BLOCK) for k in range(pair)]
            v = jnp.concatenate(
                [lv_ref[r, c].reshape(BLOCK * BLOCK, half) for c in cut], axis=1
            )
            m = jnp.dot(mix_ref[layer], v, preferred_element_type=jnp.float32) + bias
            for k, c in enumerate(cut):
                u = lu_ref[r, c].reshape(BLOCK * BLOCK, half).astype(jnp.float32)
                gated = (u * m[:, k * half : (k + 1) * half]).astype(jnp.bfloat16)
                out_ref[r, c] = gated.reshape(BLOCK, BLOCK, half)
    cells = grid_ref.shape[-1]
    wide = tiles_ref.shape[0]
    tile = wide // cells
    down_of = lax.broadcasted_iota(jnp.int32, (wide, cells), 0) // tile
    chosen = down_of == lax.broadcasted_iota(jnp.int32, (wide, cells), 1)
    shift = jnp.sum(jnp.where(chosen, grid_bias_ref[layer : layer + 1], 0.0), axis=1, keepdims=True)
    shift_ref[...] = jnp.broadcast_to(shift, shift_ref.shape)
    pick = chosen.astype(jnp.bfloat16)
    across_of = lax.broadcasted_iota(jnp.int32, (cells, wide), 1) // tile
    lay = (across_of == lax.broadcasted_iota(jnp.int32, (cells, wide), 0)).astype(jnp.bfloat16)
    tall = jnp.dot(pick, grid_ref[layer], preferred_element_type=jnp.float32)
    full = jnp.dot(tall.astype(jnp.bfloat16), lay, preferred_element_type=jnp.float32)
    p = lax.broadcasted_iota(jnp.int32, (wide, wide), 0) % tile
    q = lax.broadcasted_iota(jnp.int32, (wide, wide), 1) % tile
    tiles_ref[...] = jnp.where(p == q, full, 0.0).astype(jnp.bfloat16)


def local(layer, lu, lv, mix, bias, grid, grid_bias, tile):
    rows, cols, half = lu.shape
    wide = grid.shape[-1] * tile
    return pl.pallas_call(
        functools.partial(local_kernel, layer),
        out_shape=[
            jax.ShapeDtypeStruct(lu.shape, jnp.bfloat16),
            jax.ShapeDtypeStruct((wide, wide), jnp.bfloat16),
            jax.ShapeDtypeStruct((wide, half), jnp.float32),
        ],
        in_specs=[VMEM] * 6,
        out_specs=[VMEM] * 3,
        compiler_params=pltpu.CompilerParams(vmem_limit_bytes=12 * MIB),
        cost_estimate=pl.CostEstimate(
            flops=2 * rows * cols * half * BLOCK * BLOCK,
            bytes_accessed=6 * rows * cols * half,
            transcendentals=0,
        ),
        name="local",
    )(lu, lv, mix, bias, grid, grid_bias)


def grid_kernel(got_ref, mix_ref, bias_ref, out_ref):
    cells, share, half = got_ref.shape
    tile = mix_ref.shape[0] // cells
    step = 2 * tile if share % (2 * tile) == 0 else tile
    for k in range(share // step):
        parts = [slice(t, t + tile) for t in range(k * step, (k + 1) * step, tile)]
        if tile == 16:
            v = [got_ref[:, part].reshape(cells * tile, half) for part in parts]
        else:
            v = [
                got_ref[:, part].astype(jnp.float32).reshape(cells * tile, half).astype(jnp.bfloat16)
                for part in parts
            ]
        m = jnp.dot(
            mix_ref[...], jnp.concatenate(v, axis=1), preferred_element_type=jnp.float32
        )
        for n, part in enumerate(parts):
            blend = m[:, n * half : (n + 1) * half] + bias_ref[...]
            if tile == 16:
                out_ref[:, part] = blend.astype(jnp.bfloat16).reshape(cells, tile, half)
            else:
                out_ref[:, part] = blend.reshape(cells, tile, half).astype(jnp.bfloat16)

def grid_mixing(got, mix, bias):
    cells, share, half = got.shape
    return pl.pallas_call(
        grid_kernel,
        out_shape=jax.ShapeDtypeStruct(got.shape, jnp.bfloat16),
        in_specs=[VMEM] * 3,
        out_specs=VMEM,
        compiler_params=pltpu.CompilerParams(vmem_limit_bytes=10 * MIB),
        name="grid_mixing",
    )(got, mix, bias)


def keep_strips(top, bottom, strip_ref, near_ref, far_ref, left_ref, right_ref):
    odd_row = parity("row")

    @pl.when(odd_row == 0)
    def _():
        near_ref[...] = bottom
        far_ref[...] = top

    @pl.when(odd_row == 1)
    def _():
        near_ref[...] = top
        far_ref[...] = bottom

    left_ref[...] = strip_ref[0].astype(jnp.bfloat16)
    right_ref[...] = strip_ref[1].astype(jnp.bfloat16)


def back_kernel(layer, last, mixed_ref, gl_ref, gu_ref, gm_ref, proj_ref, cur_ref, *refs):
    rows, cols, channels = cur_ref.shape
    many = largest_divisor(rows, 8)

    @pl.loop(0, rows // many)
    def _(g):
        where = pl.ds(pl.multiple_of(g * many * cols, many * cols), many * cols)
        gated = gu_ref[where].astype(jnp.float32) * gm_ref[where].astype(jnp.float32)
        joined = jnp.concatenate([gl_ref[where], gated.astype(jnp.bfloat16)], axis=1)
        total = mixed_ref[where] + jnp.dot(
            joined, proj_ref[layer], preferred_element_type=jnp.float32
        )
        cur_ref[pl.ds(g * many, many)] = total.reshape(many, cols, channels).astype(jnp.bfloat16)
        if not last:
            strip_ref = refs[-1]
            for u in range(many):
                for c in range(RIM):
                    low = u * cols + c
                    high = (u + 1) * cols - RIM + c
                    strip_ref[0, c, pl.ds(g * many + u, 1)] = total[low : low + 1]
                    strip_ref[1, c, pl.ds(g * many + u, 1)] = total[high : high + 1]

    if not last:
        *strip_refs, strip_ref = refs
        keep_strips(cur_ref[0:RIM], cur_ref[rows - RIM : rows], strip_ref, *strip_refs)


def strip_shapes(shape):
    rows, cols, channels = shape
    return [jax.ShapeDtypeStruct((RIM, cols, channels), jnp.bfloat16)] * 2 + [
        jax.ShapeDtypeStruct((RIM, rows, channels), jnp.bfloat16)
    ] * 2


def back(layer, last, mixed, gl, gu, gm, proj, shape):
    rows, cols, channels = shape
    f32 = jnp.float32
    outs = [jax.ShapeDtypeStruct(shape, jnp.bfloat16)]
    scratch = []
    if not last:
        outs += strip_shapes(shape)
        scratch.append(pltpu.VMEM((2, RIM, rows, channels), f32))
    return pl.pallas_call(
        functools.partial(back_kernel, layer, last),
        out_shape=outs,
        in_specs=[VMEM] * 5,
        out_specs=[VMEM] * len(outs),
        scratch_shapes=scratch,
        compiler_params=pltpu.CompilerParams(vmem_limit_bytes=16 * MIB),
        cost_estimate=pl.CostEstimate(
            flops=2 * rows * cols * channels * channels,
            bytes_accessed=rows * cols * channels * 9,
            transcendentals=0,
        ),
        name="back",
    )(mixed, gl, gu, gm, proj)


def strips_kernel(image_hbm, cur_ref, *refs):
    *strip_refs, strip_ref, sem = refs
    rows, cols, channels = image_hbm.shape
    copy = pltpu.make_async_copy(image_hbm, cur_ref, sem.at[0])
    copy.start()
    copy.wait()
    side = math.gcd(cols, 16)
    for i in range(rows):
        low = cur_ref[i, 0:side].astype(jnp.float32)
        high = cur_ref[i, cols - side : cols].astype(jnp.float32)
        for c in range(RIM):
            strip_ref[0, c, i : i + 1] = low[c : c + 1]
            strip_ref[1, c, i : i + 1] = high[side - RIM + c : side - RIM + c + 1]
    keep_strips(cur_ref[0:RIM], cur_ref[rows - RIM : rows], strip_ref, *strip_refs)


def strips(image):
    rows, cols, channels = image.shape
    return pl.pallas_call(
        strips_kernel,
        out_shape=[jax.ShapeDtypeStruct(image.shape, jnp.bfloat16)] + strip_shapes(image.shape),
        in_specs=[ANY],
        out_specs=[VMEM] * 5,
        scratch_shapes=[
            pltpu.VMEM((2, RIM, rows, channels), jnp.float32),
            pltpu.SemaphoreType.DMA((1,)),
        ],
        compiler_params=pltpu.CompilerParams(vmem_limit_bytes=8 * MIB),
        name="strips",
    )(in_hbm(image))


def traded(axis, near, far):
    count = lax.axis_size(axis)
    inner = [(i, i ^ 1) for i in range(count)]
    outer = [(i, (i + 1) % count) for i in range(1, count, 2)]
    outer += [(target, source) for source, target in outer]
    far = lax.ppermute(far, axis, outer)
    near = lax.ppermute(near, axis, inner)
    return near, far


def columns_kernel(near_rows, far_rows, left_ref, right_ref, near_ref, far_ref):
    odd_row, odd_col = parity("row"), parity("col")
    rim, rows, _ = left_ref.shape
    cols = near_rows.shape[1]
    near_top = odd_row == 1
    for side, own_ref in ((0, left_ref), (1, right_ref)):
        wanted = (odd_col == 1) if side == 0 else (odd_col == 0)
        first = 0 if side == 0 else cols - rim

        def ends(rows_ref, c):
            return [rows_ref[r, first + c : first + c + 1].astype(jnp.float32) for r in range(rim)]

        strips = []
        for c in range(rim):
            close, other = ends(near_rows, c), ends(far_rows, c)
            top = [jnp.where(near_top, x, y) for x, y in zip(close, other)]
            bottom = [jnp.where(near_top, y, x) for x, y in zip(close, other)]
            strips.append(
                jnp.concatenate(top + [own_ref[c].astype(jnp.float32)] + bottom, axis=0).astype(
                    jnp.bfloat16
                )
            )

        @pl.when(wanted)
        def _():
            for c in range(rim):
                near_ref[c] = strips[c]

        @pl.when(jnp.logical_not(wanted))
        def _():
            for c in range(rim):
                far_ref[c] = strips[c]


def columns(near_rows, far_rows, left, right):
    rim, rows, channels = left.shape
    return pl.pallas_call(
        columns_kernel,
        out_shape=[jax.ShapeDtypeStruct((rim, rows + 2 * rim, channels), jnp.bfloat16)] * 2,
        in_specs=[VMEM] * 4,
        out_specs=[VMEM] * 2,
        compiler_params=pltpu.CompilerParams(vmem_limit_bytes=8 * MIB),
        name="columns",
    )(near_rows, far_rows, left, right)


def rims(near_rows, far_rows, left, right):
    rim_rows = traded("row", near_rows, far_rows)
    return rim_rows, traded("col", *columns(*rim_rows, left, right))


def on_device(
    image,
    norm_gain,
    conv_first,
    conv_second,
    proj_in,
    block_mix,
    block_bias,
    grid_mix,
    grid_bias,
    proj_out,
):
    rows, cols, channels = image.shape
    half = channels // 2
    row_count = lax.axis_size("row")
    col_count = lax.axis_size("col")
    cells = row_count * col_count
    pixels = rows * cols
    share = pixels // cells
    tile = math.gcd(share, 16)
    first = conv_first.reshape(LAYERS, 9 * channels, channels)
    second = conv_second.reshape(LAYERS, 9 * channels, channels)
    current, *own = strips(image)
    for layer in range(LAYERS):
        last = layer == LAYERS - 1
        rim_rows, rim_cols = rims(*own)
        mixed, lu, lv, gu, gv = front(
            layer, current, rim_rows, rim_cols, norm_gain, first, second, proj_in
        )
        gl, mix_tiles, bias_tiles = local(
            layer,
            lu.reshape(rows, cols, half),
            lv.reshape(rows, cols, half),
            block_mix,
            block_bias,
            grid_mix,
            grid_bias,
            tile,
        )
        gv, gl = lax.optimization_barrier((gv, gl))
        got = lax.all_to_all(
            gv.reshape(1, cells, share, half), ("row", "col"), 1, 0, tiled=True
        )
        blend = grid_mixing(got.reshape(cells, share, half), mix_tiles, bias_tiles)
        gm = lax.all_to_all(
            blend.reshape(cells, 1, share, half), ("row", "col"), 0, 1, tiled=True
        )
        current, *own = back(
            layer,
            last,
            mixed,
            gl.reshape(pixels, half),
            gu,
            gm.reshape(pixels, half),
            proj_out,
            image.shape,
        )
    return current


def solution(mesh):
    placed = (P("row", "col", None), P(), P(), P(), P(), P(), P(), P(), P(), P())
    return jax.shard_map(
        on_device, mesh=mesh, in_specs=placed, out_specs=P("row", "col", None), check_vma=False
    )
```

```python
import functools
import math

import jax
import jax.numpy as jnp
from jax import lax
from jax.experimental import pallas as pl
from jax.experimental.pallas import tpu as pltpu
from jax.sharding import PartitionSpec as P


BLOCK = 16
LAYERS = 2
RIM = 2
GROUP_ONE = 5
GROUP_TWO = 12
MIB = 1 << 20

epsilon = 1e-06
ROOT = math.sqrt(2.0 / math.pi)

VMEM = pl.BlockSpec(memory_space=pltpu.VMEM)
ANY = pl.BlockSpec(memory_space=pltpu.HBM)


def parity(axis):
    return lax.rem(lax.axis_index(axis), 2)


def edge_factors():
    factors = []
    for axis in ("row", "col"):
        place = lax.axis_index(axis)
        for end in (0, lax.axis_size(axis) - 1):
            factors.append(jnp.where(place == end, 0.0, 1.0))
    return factors


def gelu(v):
    return 0.5 * v * (1.0 + jnp.tanh(ROOT * (v + 0.044715 * (v * v * v))))


def normalised(values, gain_row):
    average = jnp.mean(values, axis=-1, keepdims=True)
    centred = values - average
    variance = jnp.mean(centred * centred, axis=-1, keepdims=True)
    return centred * lax.rsqrt(variance + epsilon) * gain_row


def rounded(values):
    return values.astype(jnp.bfloat16).astype(jnp.float32)


def largest_divisor(total, most):
    return max(d for d in range(1, most + 1) if total % d == 0)


def spread(row, left_row, right_row, dst_ref, i, cols):
    channels = row.shape[-1]
    place = lax.broadcasted_iota(jnp.int32, row.shape, 0)
    before = jnp.where(place == 0, left_row, pltpu.roll(row, 1, 0))
    after = jnp.where(place == cols - 1, right_row, pltpu.roll(row, cols - 1, 0))
    dst_ref[i, :, 0:channels] = before.astype(jnp.bfloat16)
    dst_ref[i, :, channels : 2 * channels] = row.astype(jnp.bfloat16)
    dst_ref[i, :, 2 * channels : 3 * channels] = after.astype(jnp.bfloat16)


def in_hbm(values):
    return pltpu.with_memory_space_constraint(values, pltpu.HBM)


def front_kernel(
    layer,
    cur_ref,
    near_rows,
    far_rows,
    near_cols,
    far_cols,
    gain_hbm,
    first_hbm,
    second_hbm,
    in_proj_hbm,
    mixed_ref,
    lu_ref,
    lv_ref,
    gu_ref,
    gv_ref,
    one_ref,
    two_ref,
    sides_ref,
    left_side,
    right_side,
    left_one,
    right_one,
    slot_a,
    slot_b,
    slot_c,
    slot_d,
    first_ref,
    second_ref,
    in_ref,
    gain_ref,
    sems,
):
    rows, cols, channels = cur_ref.shape
    feed = [
        pltpu.make_async_copy(src.at[layer], dst, sems.at[k])
        for k, (src, dst) in enumerate(
            ((first_hbm, first_ref), (second_hbm, second_ref), (in_proj_hbm, in_ref))
        )
    ]
    gain_copy = pltpu.make_async_copy(gain_hbm.at[layer], gain_ref, sems.at[3])
    gain_copy.start()
    for copy in feed:
        copy.start()
    half = channels // 2
    near_top = parity("row") == 1
    near_left = parity("col") == 1
    edge_ref = edge_factors()
    gain_copy.wait()
    gain_one = gain_ref[0:1, :]
    gain_two = gain_ref[1:2, :]
    long = rows + 2 * RIM

    spot = lax.broadcasted_iota(jnp.int32, (long, channels), 0)
    within = jnp.where(spot < RIM, edge_ref[0], jnp.where(spot < long - RIM, 1.0, edge_ref[1]))

    def chosen(near_low, side, near, far):
        low, high = (near, far) if side == 0 else (far, near)
        return jnp.where(near_low, low.astype(jnp.float32), high.astype(jnp.float32))

    for side in range(2):
        for c in range(RIM):
            sides_ref[side * RIM + c, 0:long] = rounded(
                normalised(chosen(near_left, side, near_cols[c], far_cols[c]), gain_one)
            ) * (within * edge_ref[2 + side])
    left_side[0:long, 0:channels] = sides_ref[0, 0:long]
    left_side[0:long, channels : 2 * channels] = sides_ref[1, 0:long]
    right_side[0:long, channels : 2 * channels] = sides_ref[2, 0:long]
    right_side[0:long, 2 * channels : 3 * channels] = sides_ref[3, 0:long]

    def norm_row(values, dst, keep=None):
        row = rounded(normalised(values, gain_one))
        if keep is not None:
            row = row * keep
        spread(row, sides_ref[1, dst : dst + 1], sides_ref[2, dst : dst + 1], one_ref, dst, cols)
        left_side[dst : dst + 1, 2 * channels : 3 * channels] = row[0:1]
        right_side[dst : dst + 1, 0:channels] = row[cols - 1 : cols]

    def norm_any(dst):
        if dst < RIM:
            norm_row(chosen(near_top, 0, near_rows[dst], far_rows[dst]), dst, edge_ref[0])
        elif dst < RIM + rows:
            norm_row(cur_ref[dst - RIM].astype(jnp.float32), dst)
        else:
            r = dst - RIM - rows
            norm_row(chosen(near_top, 1, near_rows[r], far_rows[r]), dst, edge_ref[1])

    def windows(src_ref, base, count):
        return jnp.concatenate(
            [
                src_ref[pl.ds(base + a, count)].reshape(count * cols, 3 * channels)
                for a in range(3)
            ],
            axis=1,
        )

    tall = rows + 2
    group = slot_a.shape[0] // cols
    first_steps = tall // group
    ends = -(-group // 16) * 16

    def first_multiply(g, slot):
        base = g * group
        sides = [
            jnp.concatenate([side[base + a : base + a + ends] for a in range(3)], axis=1)
            for side in (left_side, right_side)
        ]
        window = jnp.concatenate(
            [windows(one_ref, base, group)] + [v.astype(jnp.bfloat16) for v in sides], axis=0
        )
        total = jnp.dot(window, first_ref[...], preferred_element_type=jnp.float32)
        slot[...] = total[: group * cols]
        place = lax.broadcasted_iota(jnp.int32, (ends, channels), 0) + base
        inside = jnp.where(place == 0, edge_ref[0], jnp.where(place == tall - 1, edge_ref[1], 1.0))
        for k, one_side in enumerate((left_one, right_one)):
            start = group * cols + k * ends
            part = rounded(gelu(total[start : start + ends]) * (inside * edge_ref[2 + k]))
            one_side[base : base + group] = part[:group]

    def first_finish(g, slot):
        for u in range(group):
            i = g * group + u
            row = rounded(gelu(slot[u * cols : (u + 1) * cols]))
            if i == 0:
                row = row * edge_ref[0]
            if i == tall - 1:
                row = row * edge_ref[1]
            spread(row, left_one[i : i + 1], right_one[i : i + 1], two_ref, i, cols)

    many = slot_c.shape[0] // cols

    def second_multiply(g, slot):
        slot[...] = jnp.dot(
            windows(two_ref, g * many, many),
            second_ref[...],
            preferred_element_type=jnp.float32,
        )

    def second_finish(g, slot):
        where = slice(g * many * cols, (g + 1) * many * cols)
        total = slot[...] + cur_ref[pl.ds(g * many, many)].reshape(
            many * cols, channels
        ).astype(jnp.float32)
        mixed_ref[where] = total
        normed = normalised(total, gain_two).astype(jnp.bfloat16)
        expanded = gelu(
            jnp.dot(normed, in_ref[...], preferred_element_type=jnp.float32)
        ).astype(jnp.bfloat16)
        for k, out in enumerate((lu_ref, lv_ref, gu_ref, gv_ref)):
            out[where] = expanded[:, k * half : (k + 1) * half]

    second_steps = rows // many
    slots = (slot_a, slot_b)
    others = (slot_c, slot_d)

    def norm_group(g):
        begin = 0 if g == 0 else g * group + 2
        for dst in range(begin, (g + 1) * group + 2):
            norm_any(dst)

    norm_group(0)
    feed[0].wait()
    for g in range(first_steps):
        first_multiply(g, slots[g % 2])
        if g > 0:
            first_finish(g - 1, slots[(g - 1) % 2])
        if g + 1 < first_steps:
            norm_group(g + 1)
    feed[1].wait()
    feed[2].wait()
    second_multiply(0, others[0])
    first_finish(first_steps - 1, slots[(first_steps - 1) % 2])
    for g in range(1, second_steps):
        second_multiply(g, others[g % 2])
        second_finish(g - 1, others[(g - 1) % 2])
    second_finish(second_steps - 1, others[(second_steps - 1) % 2])


def front(layer, cur, rim_rows, rim_cols, gains, first, second, proj):
    rows, cols, channels = cur.shape
    pixels = rows * cols
    half = channels // 2
    long = rows + 2 * RIM
    tall = -(-(rows + 2) // 16) * 16 + 16
    group = largest_divisor(rows + 2, GROUP_ONE)
    many = largest_divisor(rows, GROUP_TWO)
    bf = jnp.bfloat16
    f32 = jnp.float32
    outs = [jax.ShapeDtypeStruct((pixels, channels), f32)]
    outs += [jax.ShapeDtypeStruct((pixels, half), bf)] * 4
    return pl.pallas_call(
        functools.partial(front_kernel, layer),
        out_shape=outs,
        in_specs=[VMEM] * 5 + [ANY] * 4,
        out_specs=[VMEM] * 5,
        scratch_shapes=[
            pltpu.VMEM((long, cols, 3 * channels), bf),
            pltpu.VMEM((rows + 2, cols, 3 * channels), bf),
            pltpu.VMEM((2 * RIM, tall, channels), f32),
            pltpu.VMEM((tall, 3 * channels), f32),
            pltpu.VMEM((tall, 3 * channels), f32),
            pltpu.VMEM((rows + 2, channels), f32),
            pltpu.VMEM((rows + 2, channels), f32),
            pltpu.VMEM((group * cols, channels), f32),
            pltpu.VMEM((group * cols, channels), f32),
            pltpu.VMEM((many * cols, channels), f32),
            pltpu.VMEM((many * cols, channels), f32),
            pltpu.VMEM(first.shape[1:], bf),
            pltpu.VMEM(second.shape[1:], bf),
            pltpu.VMEM(proj.shape[1:], bf),
            pltpu.VMEM(gains.shape[1:], f32),
            pltpu.SemaphoreType.DMA((4,)),
        ],
        compiler_params=pltpu.CompilerParams(vmem_limit_bytes=34 * MIB),
        cost_estimate=pl.CostEstimate(
            flops=2 * pixels * channels * channels * 20,
            bytes_accessed=12 << 20,
            transcendentals=3 * pixels * channels,
        ),
        name="front",
    )(cur, *rim_rows, *rim_cols, *(in_hbm(w) for w in (gains, first, second, proj)))


def local_kernel(
    layer, lu_ref, lv_ref, mix_ref, bias_ref, grid_ref, grid_bias_ref, out_ref, tiles_ref, shift_ref
):
    rows, cols, half = lu_ref.shape
    down, across = rows // BLOCK, cols // BLOCK
    pair = 2 if across % 2 == 0 else 1
    area = BLOCK * BLOCK
    spot = lax.broadcasted_iota(jnp.int32, (area, area), 0)
    same = spot == lax.broadcasted_iota(jnp.int32, (area, area), 1)
    bias = jnp.sum(jnp.where(same, bias_ref[layer : layer + 1], 0.0), axis=1, keepdims=True)
    for i in range(down):
        r = slice(i * BLOCK, (i + 1) * BLOCK)
        for j in range(0, across, pair):
            cut = [slice((j + k) * BLOCK, (j + k + 1) * BLOCK) for k in range(pair)]
            v = jnp.concatenate(
                [lv_ref[r, c].reshape(BLOCK * BLOCK, half) for c in cut], axis=1
            )
            m = jnp.dot(mix_ref[layer], v, preferred_element_type=jnp.float32) + bias
            for k, c in enumerate(cut):
                u = lu_ref[r, c].reshape(BLOCK * BLOCK, half).astype(jnp.float32)
                gated = (u * m[:, k * half : (k + 1) * half]).astype(jnp.bfloat16)
                out_ref[r, c] = gated.reshape(BLOCK, BLOCK, half)
    cells = grid_ref.shape[-1]
    wide = tiles_ref.shape[0]
    tile = wide // cells
    down_of = lax.broadcasted_iota(jnp.int32, (wide, cells), 0) // tile
    chosen = down_of == lax.broadcasted_iota(jnp.int32, (wide, cells), 1)
    shift = jnp.sum(jnp.where(chosen, grid_bias_ref[layer : layer + 1], 0.0), axis=1, keepdims=True)
    shift_ref[...] = jnp.broadcast_to(shift, shift_ref.shape)
    pick = chosen.astype(jnp.bfloat16)
    across_of = lax.broadcasted_iota(jnp.int32, (cells, wide), 1) // tile
    lay = (across_of == lax.broadcasted_iota(jnp.int32, (cells, wide), 0)).astype(jnp.bfloat16)
    tall = jnp.dot(pick, grid_ref[layer], preferred_element_type=jnp.float32)
    full = jnp.dot(tall.astype(jnp.bfloat16), lay, preferred_element_type=jnp.float32)
    p = lax.broadcasted_iota(jnp.int32, (wide, wide), 0) % tile
    q = lax.broadcasted_iota(jnp.int32, (wide, wide), 1) % tile
    tiles_ref[...] = jnp.where(p == q, full, 0.0).astype(jnp.bfloat16)


def local(layer, lu, lv, mix, bias, grid, grid_bias, tile):
    rows, cols, half = lu.shape
    wide = grid.shape[-1] * tile
    return pl.pallas_call(
        functools.partial(local_kernel, layer),
        out_shape=[
            jax.ShapeDtypeStruct(lu.shape, jnp.bfloat16),
            jax.ShapeDtypeStruct((wide, wide), jnp.bfloat16),
            jax.ShapeDtypeStruct((wide, half), jnp.float32),
        ],
        in_specs=[VMEM] * 6,
        out_specs=[VMEM] * 3,
        compiler_params=pltpu.CompilerParams(vmem_limit_bytes=12 * MIB),
        cost_estimate=pl.CostEstimate(
            flops=2 * rows * cols * half * BLOCK * BLOCK,
            bytes_accessed=6 * rows * cols * half,
            transcendentals=0,
        ),
        name="local",
    )(lu, lv, mix, bias, grid, grid_bias)


def grid_kernel(got_ref, mix_ref, bias_ref, out_ref):
    cells, share, half = got_ref.shape
    tile = mix_ref.shape[0] // cells
    step = 2 * tile if share % (2 * tile) == 0 else tile
    for k in range(share // step):
        parts = [slice(t, t + tile) for t in range(k * step, (k + 1) * step, tile)]
        if tile == 16:
            v = [got_ref[:, part].reshape(cells * tile, half) for part in parts]
        else:
            v = [
                got_ref[:, part].astype(jnp.float32).reshape(cells * tile, half).astype(jnp.bfloat16)
                for part in parts
            ]
        m = jnp.dot(
            mix_ref[...], jnp.concatenate(v, axis=1), preferred_element_type=jnp.float32
        )
        for n, part in enumerate(parts):
            blend = m[:, n * half : (n + 1) * half] + bias_ref[...]
            if tile == 16:
                out_ref[:, part] = blend.astype(jnp.bfloat16).reshape(cells, tile, half)
            else:
                out_ref[:, part] = blend.reshape(cells, tile, half).astype(jnp.bfloat16)


def grid_mixing(got, mix, bias):
    return pl.pallas_call(
        grid_kernel,
        out_shape=jax.ShapeDtypeStruct(got.shape, jnp.bfloat16),
        in_specs=[VMEM] * 3,
        out_specs=VMEM,
        compiler_params=pltpu.CompilerParams(vmem_limit_bytes=10 * MIB),
        name="grid_mixing",
    )(got, mix, bias)


def keep_strips(top, bottom, strip_ref, near_ref, far_ref, left_ref, right_ref):
    odd_row = parity("row")

    @pl.when(odd_row == 0)
    def _():
        near_ref[...] = bottom
        far_ref[...] = top

    @pl.when(odd_row == 1)
    def _():
        near_ref[...] = top
        far_ref[...] = bottom

    left_ref[...] = strip_ref[0].astype(jnp.bfloat16)
    right_ref[...] = strip_ref[1].astype(jnp.bfloat16)


def back_kernel(layer, last, mixed_ref, gl_ref, gu_ref, gm_ref, proj_ref, cur_ref, *refs):
    rows, cols, channels = cur_ref.shape
    many = largest_divisor(rows, 8)

    @pl.loop(0, rows // many)
    def _(g):
        where = pl.ds(pl.multiple_of(g * many * cols, many * cols), many * cols)
        gated = gu_ref[where].astype(jnp.float32) * gm_ref[where].astype(jnp.float32)
        joined = jnp.concatenate([gl_ref[where], gated.astype(jnp.bfloat16)], axis=1)
        total = mixed_ref[where] + jnp.dot(
            joined, proj_ref[layer], preferred_element_type=jnp.float32
        )
        cur_ref[pl.ds(g * many, many)] = total.reshape(many, cols, channels).astype(jnp.bfloat16)
        if not last:
            strip_ref = refs[-1]
            for u in range(many):
                for c in range(RIM):
                    low = u * cols + c
                    high = (u + 1) * cols - RIM + c
                    strip_ref[0, c, pl.ds(g * many + u, 1)] = total[low : low + 1]
                    strip_ref[1, c, pl.ds(g * many + u, 1)] = total[high : high + 1]

    if not last:
        *strip_refs, strip_ref = refs
        keep_strips(cur_ref[0:RIM], cur_ref[rows - RIM : rows], strip_ref, *strip_refs)


def strip_shapes(shape):
    rows, cols, channels = shape
    return [jax.ShapeDtypeStruct((RIM, cols, channels), jnp.bfloat16)] * 2 + [
        jax.ShapeDtypeStruct((RIM, rows, channels), jnp.bfloat16)
    ] * 2


def back(layer, last, mixed, gl, gu, gm, proj, shape):
    rows, cols, channels = shape
    f32 = jnp.float32
    outs = [jax.ShapeDtypeStruct(shape, jnp.bfloat16)]
    scratch = []
    if not last:
        outs += strip_shapes(shape)
        scratch.append(pltpu.VMEM((2, RIM, rows, channels), f32))
    return pl.pallas_call(
        functools.partial(back_kernel, layer, last),
        out_shape=outs,
        in_specs=[VMEM] * 5,
        out_specs=[VMEM] * len(outs),
        scratch_shapes=scratch,
        compiler_params=pltpu.CompilerParams(vmem_limit_bytes=16 * MIB),
        cost_estimate=pl.CostEstimate(
            flops=2 * rows * cols * channels * channels,
            bytes_accessed=rows * cols * channels * 9,
            transcendentals=0,
        ),
        name="back",
    )(mixed, gl, gu, gm, proj)


def strips_kernel(image_hbm, cur_ref, *refs):
    *strip_refs, strip_ref, sem = refs
    rows, cols, _ = image_hbm.shape
    copy = pltpu.make_async_copy(image_hbm, cur_ref, sem.at[0])
    copy.start()
    copy.wait()
    side = math.gcd(cols, 16)
    for i in range(rows):
        low = cur_ref[i, 0:side].astype(jnp.float32)
        high = cur_ref[i, cols - side : cols].astype(jnp.float32)
        for c in range(RIM):
            strip_ref[0, c, i : i + 1] = low[c : c + 1]
            strip_ref[1, c, i : i + 1] = high[side - RIM + c : side - RIM + c + 1]
    keep_strips(cur_ref[0:RIM], cur_ref[rows - RIM : rows], strip_ref, *strip_refs)


def strips(image):
    rows, _, channels = image.shape
    return pl.pallas_call(
        strips_kernel,
        out_shape=[jax.ShapeDtypeStruct(image.shape, jnp.bfloat16)] + strip_shapes(image.shape),
        in_specs=[ANY],
        out_specs=[VMEM] * 5,
        scratch_shapes=[
            pltpu.VMEM((2, RIM, rows, channels), jnp.float32),
            pltpu.SemaphoreType.DMA((1,)),
        ],
        compiler_params=pltpu.CompilerParams(vmem_limit_bytes=8 * MIB),
        name="strips",
    )(in_hbm(image))


def traded(axis, near, far, around):
    count = lax.axis_size(axis)
    inner = [(i, i ^ 1) for i in range(count)]
    outer = [(i, (i + 1) % count) for i in range(1, count if around else count - 1, 2)]
    outer += [(target, source) for source, target in outer]
    far = lax.ppermute(far, axis, outer)
    near = lax.ppermute(near, axis, inner)
    return near, far


def columns_kernel(near_rows, far_rows, left_ref, right_ref, near_ref, far_ref):
    odd_row, odd_col = parity("row"), parity("col")
    rim, _, _ = left_ref.shape
    cols = near_rows.shape[1]
    near_top = odd_row == 1
    for side, own_ref in ((0, left_ref), (1, right_ref)):
        wanted = (odd_col == 1) if side == 0 else (odd_col == 0)
        first = 0 if side == 0 else cols - rim

        def ends(rows_ref, c):
            return [rows_ref[r, first + c : first + c + 1].astype(jnp.float32) for r in range(rim)]

        strips = []
        for c in range(rim):
            close, other = ends(near_rows, c), ends(far_rows, c)
            top = [jnp.where(near_top, x, y) for x, y in zip(close, other)]
            bottom = [jnp.where(near_top, y, x) for x, y in zip(close, other)]
            strips.append(
                jnp.concatenate(top + [own_ref[c].astype(jnp.float32)] + bottom, axis=0).astype(
                    jnp.bfloat16
                )
            )

        @pl.when(wanted)
        def _():
            for c in range(rim):
                near_ref[c] = strips[c]

        @pl.when(jnp.logical_not(wanted))
        def _():
            for c in range(rim):
                far_ref[c] = strips[c]


def columns(near_rows, far_rows, left, right):
    rim, rows, channels = left.shape
    return pl.pallas_call(
        columns_kernel,
        out_shape=[jax.ShapeDtypeStruct((rim, rows + 2 * rim, channels), jnp.bfloat16)] * 2,
        in_specs=[VMEM] * 4,
        out_specs=[VMEM] * 2,
        compiler_params=pltpu.CompilerParams(vmem_limit_bytes=8 * MIB),
        name="columns",
    )(near_rows, far_rows, left, right)


def rims(near_rows, far_rows, left, right):
    rim_rows = traded("row", near_rows, far_rows, True)
    return rim_rows, traded("col", *columns(*rim_rows, left, right), False)


def on_device(
    image,
    norm_gain,
    conv_first,
    conv_second,
    proj_in,
    block_mix,
    block_bias,
    grid_mix,
    grid_bias,
    proj_out,
):
    rows, cols, channels = image.shape
    half = channels // 2
    row_count = lax.axis_size("row")
    col_count = lax.axis_size("col")
    cells = row_count * col_count
    pixels = rows * cols
    share = pixels // cells
    tile = math.gcd(share, 16)
    first = conv_first.reshape(LAYERS, 9 * channels, channels)
    second = conv_second.reshape(LAYERS, 9 * channels, channels)
    current, *own = strips(image)
    for layer in range(LAYERS):
        last = layer == LAYERS - 1
        rim_rows, rim_cols = rims(*own)
        mixed, lu, lv, gu, gv = front(
            layer, current, rim_rows, rim_cols, norm_gain, first, second, proj_in
        )
        gl, mix_tiles, bias_tiles = local(
            layer,
            lu.reshape(rows, cols, half),
            lv.reshape(rows, cols, half),
            block_mix,
            block_bias,
            grid_mix,
            grid_bias,
            tile,
        )
        gv, gl = lax.optimization_barrier((gv, gl))
        got = lax.all_to_all(gv.reshape(1, cells, share, half), ("row", "col"), 1, 0, tiled=True)
        blend = grid_mixing(got.reshape(cells, share, half), mix_tiles, bias_tiles)
        gm = lax.all_to_all(blend.reshape(cells, 1, share, half), ("row", "col"), 0, 1, tiled=True)
        current, *own = back(
            layer,
            last,
            mixed,
            gl.reshape(pixels, half),
            gu,
            gm.reshape(pixels, half),
            proj_out,
            image.shape,
        )
    return current


def solution(mesh):
    placed = (P("row", "col", None), P(), P(), P(), P(), P(), P(), P(), P(), P())
    return jax.shard_map(
        on_device, mesh=mesh, in_specs=placed, out_specs=P("row", "col", None), check_vma=False
    )
```

```python
import functools
import math

import jax
import jax.numpy as jnp
from jax import lax
from jax.experimental import pallas as pl
from jax.experimental.pallas import tpu as pltpu
from jax.sharding import PartitionSpec as P


BLOCK = 16
LAYERS = 2
RIM = 2
GROUP_ONE = 5
GROUP_TWO = 12
MIB = 1 << 20

epsilon = 1e-06
ROOT = math.sqrt(2.0 / math.pi)

VMEM = pl.BlockSpec(memory_space=pltpu.VMEM)
ANY = pl.BlockSpec(memory_space=pltpu.HBM)


def parity(axis):
    return lax.rem(lax.axis_index(axis), 2)


def edge_factors():
    factors = []
    for axis in ("row", "col"):
        place = lax.axis_index(axis)
        for end in (0, lax.axis_size(axis) - 1):
            factors.append(jnp.where(place == end, 0.0, 1.0))
    return factors


def gelu(v):
    return 0.5 * v * (1.0 + jnp.tanh(ROOT * (v + 0.044715 * (v * v * v))))


def normalised(values, gain_row):
    average = jnp.mean(values, axis=-1, keepdims=True)
    centred = values - average
    variance = jnp.mean(centred * centred, axis=-1, keepdims=True)
    return centred * lax.rsqrt(variance + epsilon) * gain_row


def rounded(values):
    return values.astype(jnp.bfloat16).astype(jnp.float32)


def largest_divisor(total, most):
    return max(d for d in range(1, most + 1) if total % d == 0)


def spread(row, left_row, right_row, dst_ref, i, cols):
    channels = row.shape[-1]
    place = lax.broadcasted_iota(jnp.int32, row.shape, 0)
    before = jnp.where(place == 0, left_row, pltpu.roll(row, 1, 0))
    after = jnp.where(place == cols - 1, right_row, pltpu.roll(row, cols - 1, 0))
    dst_ref[i, :, 0:channels] = before.astype(jnp.bfloat16)
    dst_ref[i, :, channels : 2 * channels] = row.astype(jnp.bfloat16)
    dst_ref[i, :, 2 * channels : 3 * channels] = after.astype(jnp.bfloat16)


def in_hbm(values):
    return pltpu.with_memory_space_constraint(values, pltpu.HBM)


def front_kernel(
    layer,
    cur_ref,
    near_rows,
    far_rows,
    near_cols,
    far_cols,
    gain_hbm,
    first_hbm,
    second_hbm,
    in_proj_hbm,
    mixed_ref,
    lu_ref,
    lv_ref,
    gu_ref,
    gv_ref,
    one_ref,
    two_ref,
    sides_ref,
    left_side,
    right_side,
    left_one,
    right_one,
    slot_a,
    slot_b,
    slot_c,
    slot_d,
    first_ref,
    second_ref,
    in_ref,
    gain_ref,
    sems,
):
    rows, cols, channels = cur_ref.shape
    feed = [
        pltpu.make_async_copy(src.at[layer], dst, sems.at[k])
        for k, (src, dst) in enumerate(
            ((first_hbm, first_ref), (second_hbm, second_ref), (in_proj_hbm, in_ref))
        )
    ]
    gain_copy = pltpu.make_async_copy(gain_hbm.at[layer], gain_ref, sems.at[3])
    gain_copy.start()
    for copy in feed:
        copy.start()
    half = channels // 2
    near_top = parity("row") == 1
    near_left = parity("col") == 1
    edge_ref = edge_factors()
    gain_copy.wait()
    gain_one = gain_ref[0:1, :]
    gain_two = gain_ref[1:2, :]
    long = rows + 2 * RIM

    spot = lax.broadcasted_iota(jnp.int32, (long, channels), 0)
    within = jnp.where(spot < RIM, edge_ref[0], jnp.where(spot < long - RIM, 1.0, edge_ref[1]))

    def chosen(near_low, side, near, far):
        low, high = (near, far) if side == 0 else (far, near)
        return jnp.where(near_low, low.astype(jnp.float32), high.astype(jnp.float32))

    for side in range(2):
        for c in range(RIM):
            sides_ref[side * RIM + c, 0:long] = rounded(
                normalised(chosen(near_left, side, near_cols[c], far_cols[c]), gain_one)
            ) * (within * edge_ref[2 + side])
    left_side[0:long, 0:channels] = sides_ref[0, 0:long]
    left_side[0:long, channels : 2 * channels] = sides_ref[1, 0:long]
    right_side[0:long, channels : 2 * channels] = sides_ref[2, 0:long]
    right_side[0:long, 2 * channels : 3 * channels] = sides_ref[3, 0:long]

    def norm_row(values, dst, keep=None):
        row = rounded(normalised(values, gain_one))
        if keep is not None:
            row = row * keep
        spread(row, sides_ref[1, dst : dst + 1], sides_ref[2, dst : dst + 1], one_ref, dst, cols)
        left_side[dst : dst + 1, 2 * channels : 3 * channels] = row[0:1]
        right_side[dst : dst + 1, 0:channels] = row[cols - 1 : cols]

    def norm_any(dst):
        if dst < RIM:
            norm_row(chosen(near_top, 0, near_rows[dst], far_rows[dst]), dst, edge_ref[0])
        elif dst < RIM + rows:
            norm_row(cur_ref[dst - RIM].astype(jnp.float32), dst)
        else:
            r = dst - RIM - rows
            norm_row(chosen(near_top, 1, near_rows[r], far_rows[r]), dst, edge_ref[1])

    def windows(src_ref, base, count):
        return jnp.concatenate(
            [
                src_ref[pl.ds(base + a, count)].reshape(count * cols, 3 * channels)
                for a in range(3)
            ],
            axis=1,
        )

    tall = rows + 2
    group = slot_a.shape[0] // cols
    first_steps = tall // group
    ends = -(-group // 16) * 16

    def first_multiply(g, slot):
        base = g * group
        sides = [
            jnp.concatenate([side[base + a : base + a + ends] for a in range(3)], axis=1)
            for side in (left_side, right_side)
        ]
        window = jnp.concatenate(
            [windows(one_ref, base, group)] + [v.astype(jnp.bfloat16) for v in sides], axis=0
        )
        total = jnp.dot(window, first_ref[...], preferred_element_type=jnp.float32)
        slot[...] = total[: group * cols]
        place = lax.broadcasted_iota(jnp.int32, (ends, channels), 0) + base
        inside = jnp.where(place == 0, edge_ref[0], jnp.where(place == tall - 1, edge_ref[1], 1.0))
        for k, one_side in enumerate((left_one, right_one)):
            start = group * cols + k * ends
            part = rounded(gelu(total[start : start + ends]) * (inside * edge_ref[2 + k]))
            one_side[base : base + group] = part[:group]

    def first_finish(g, slot):
        for u in range(group):
            i = g * group + u
            row = rounded(gelu(slot[u * cols : (u + 1) * cols]))
            if i == 0:
                row = row * edge_ref[0]
            if i == tall - 1:
                row = row * edge_ref[1]
            spread(row, left_one[i : i + 1], right_one[i : i + 1], two_ref, i, cols)

    many = slot_c.shape[0] // cols

    def second_multiply(g, slot):
        slot[...] = jnp.dot(
            windows(two_ref, g * many, many),
            second_ref[...],
            preferred_element_type=jnp.float32,
        )

    def second_finish(g, slot):
        where = slice(g * many * cols, (g + 1) * many * cols)
        total = slot[...] + cur_ref[pl.ds(g * many, many)].reshape(
            many * cols, channels
        ).astype(jnp.float32)
        mixed_ref[where] = total
        normed = normalised(total, gain_two).astype(jnp.bfloat16)
        expanded = gelu(
            jnp.dot(normed, in_ref[...], preferred_element_type=jnp.float32)
        ).astype(jnp.bfloat16)
        for k, out in enumerate((lu_ref, lv_ref, gu_ref, gv_ref)):
            out[where] = expanded[:, k * half : (k + 1) * half]

    second_steps = rows // many
    slots = (slot_a, slot_b)
    others = (slot_c, slot_d)

    def norm_group(g):
        begin = 0 if g == 0 else g * group + 2
        for dst in range(begin, (g + 1) * group + 2):
            norm_any(dst)

    norm_group(0)
    feed[0].wait()
    for g in range(first_steps):
        first_multiply(g, slots[g % 2])
        if g > 0:
            first_finish(g - 1, slots[(g - 1) % 2])
        if g + 1 < first_steps:
            norm_group(g + 1)
    feed[1].wait()
    feed[2].wait()
    second_multiply(0, others[0])
    first_finish(first_steps - 1, slots[(first_steps - 1) % 2])
    for g in range(1, second_steps):
        second_multiply(g, others[g % 2])
        second_finish(g - 1, others[(g - 1) % 2])
    second_finish(second_steps - 1, others[(second_steps - 1) % 2])


def front(layer, cur, rim_rows, rim_cols, gains, first, second, proj):
    rows, cols, channels = cur.shape
    pixels = rows * cols
    half = channels // 2
    long = rows + 2 * RIM
    tall = -(-(rows + 2) // 16) * 16 + 16
    group = largest_divisor(rows + 2, GROUP_ONE)
    many = largest_divisor(rows, GROUP_TWO)
    bf = jnp.bfloat16
    f32 = jnp.float32
    outs = [jax.ShapeDtypeStruct((pixels, channels), f32)]
    outs += [jax.ShapeDtypeStruct((pixels, half), bf)] * 4
    return pl.pallas_call(
        functools.partial(front_kernel, layer),
        out_shape=outs,
        in_specs=[VMEM] * 5 + [ANY] * 4,
        out_specs=[VMEM] * 5,
        scratch_shapes=[
            pltpu.VMEM((long, cols, 3 * channels), bf),
            pltpu.VMEM((rows + 2, cols, 3 * channels), bf),
            pltpu.VMEM((2 * RIM, tall, channels), f32),
            pltpu.VMEM((tall, 3 * channels), f32),
            pltpu.VMEM((tall, 3 * channels), f32),
            pltpu.VMEM((rows + 2, channels), f32),
            pltpu.VMEM((rows + 2, channels), f32),
            pltpu.VMEM((group * cols, channels), f32),
            pltpu.VMEM((group * cols, channels), f32),
            pltpu.VMEM((many * cols, channels), f32),
            pltpu.VMEM((many * cols, channels), f32),
            pltpu.VMEM(first.shape[1:], bf),
            pltpu.VMEM(second.shape[1:], bf),
            pltpu.VMEM(proj.shape[1:], bf),
            pltpu.VMEM(gains.shape[1:], f32),
            pltpu.SemaphoreType.DMA((4,)),
        ],
        compiler_params=pltpu.CompilerParams(vmem_limit_bytes=34 * MIB),
        cost_estimate=pl.CostEstimate(
            flops=2 * pixels * channels * channels * 20,
            bytes_accessed=12 << 20,
            transcendentals=3 * pixels * channels,
        ),
        name="front",
    )(cur, *rim_rows, *rim_cols, *(in_hbm(w) for w in (gains, first, second, proj)))


def local_kernel(layer, lu_ref, lv_ref, mix_ref, bias_ref, out_ref):
    rows, cols, half = lu_ref.shape
    down, across = rows // BLOCK, cols // BLOCK
    pair = 2 if across % 2 == 0 else 1
    area = BLOCK * BLOCK
    spot = lax.broadcasted_iota(jnp.int32, (area, area), 0)
    same = spot == lax.broadcasted_iota(jnp.int32, (area, area), 1)
    bias = jnp.sum(jnp.where(same, bias_ref[layer : layer + 1], 0.0), axis=1, keepdims=True)
    for i in range(down):
        r = slice(i * BLOCK, (i + 1) * BLOCK)
        for j in range(0, across, pair):
            cut = [slice((j + k) * BLOCK, (j + k + 1) * BLOCK) for k in range(pair)]
            v = jnp.concatenate(
                [lv_ref[r, c].reshape(BLOCK * BLOCK, half) for c in cut], axis=1
            )
            m = jnp.dot(mix_ref[layer], v, preferred_element_type=jnp.float32) + bias
            for k, c in enumerate(cut):
                u = lu_ref[r, c].reshape(BLOCK * BLOCK, half).astype(jnp.float32)
                gated = (u * m[:, k * half : (k + 1) * half]).astype(jnp.bfloat16)
                out_ref[r, c] = gated.reshape(BLOCK, BLOCK, half)


def tiles_kernel(grid_ref, grid_bias_ref, tiles_ref, shift_ref):
    cells = grid_ref.shape[-1]
    wide = tiles_ref.shape[1]
    tile = wide // cells
    down_of = lax.broadcasted_iota(jnp.int32, (wide, cells), 0) // tile
    chosen = down_of == lax.broadcasted_iota(jnp.int32, (wide, cells), 1)
    for layer in range(grid_ref.shape[0]):
        shift = jnp.sum(jnp.where(chosen, grid_bias_ref[layer : layer + 1], 0.0), axis=1, keepdims=True)
        shift_ref[layer] = jnp.broadcast_to(shift, shift_ref.shape[1:])
        pick = chosen.astype(jnp.bfloat16)
        across_of = lax.broadcasted_iota(jnp.int32, (cells, wide), 1) // tile
        lay = (across_of == lax.broadcasted_iota(jnp.int32, (cells, wide), 0)).astype(jnp.bfloat16)
        tall = jnp.dot(pick, grid_ref[layer], preferred_element_type=jnp.float32)
        full = jnp.dot(tall.astype(jnp.bfloat16), lay, preferred_element_type=jnp.float32)
        p = lax.broadcasted_iota(jnp.int32, (wide, wide), 0) % tile
        q = lax.broadcasted_iota(jnp.int32, (wide, wide), 1) % tile
        tiles_ref[layer] = jnp.where(p == q, full, 0.0).astype(jnp.bfloat16)


def mixing_tiles(grid, grid_bias, tile, half):
    layers, cells, _ = grid.shape
    wide = cells * tile
    return pl.pallas_call(
        tiles_kernel,
        out_shape=[
            jax.ShapeDtypeStruct((layers, wide, wide), jnp.bfloat16),
            jax.ShapeDtypeStruct((layers, wide, half), jnp.float32),
        ],
        in_specs=[VMEM] * 2,
        out_specs=[VMEM] * 2,
        compiler_params=pltpu.CompilerParams(vmem_limit_bytes=24 * MIB),
        cost_estimate=pl.CostEstimate(flops=0, bytes_accessed=4 * MIB, transcendentals=0),
        name="mixing_tiles",
    )(grid, grid_bias)


def local(layer, lu, lv, mix, bias):
    rows, cols, half = lu.shape
    return pl.pallas_call(
        functools.partial(local_kernel, layer),
        out_shape=jax.ShapeDtypeStruct(lu.shape, jnp.bfloat16),
        in_specs=[VMEM] * 4,
        out_specs=VMEM,
        compiler_params=pltpu.CompilerParams(vmem_limit_bytes=12 * MIB),
        cost_estimate=pl.CostEstimate(
            flops=2 * rows * cols * half * BLOCK * BLOCK,
            bytes_accessed=6 * rows * cols * half,
            transcendentals=0,
        ),
        name="local",
    )(lu, lv, mix, bias)


def grid_kernel(layer, got_ref, mix_ref, bias_ref, out_ref):
    cells, share, half = got_ref.shape
    tile = mix_ref.shape[1] // cells
    step = 2 * tile if share % (2 * tile) == 0 else tile
    for k in range(share // step):
        parts = [slice(t, t + tile) for t in range(k * step, (k + 1) * step, tile)]
        if tile == 16:
            v = [got_ref[:, part].reshape(cells * tile, half) for part in parts]
        else:
            v = [
                got_ref[:, part].astype(jnp.float32).reshape(cells * tile, half).astype(jnp.bfloat16)
                for part in parts
            ]
        m = jnp.dot(
            mix_ref[layer], jnp.concatenate(v, axis=1), preferred_element_type=jnp.float32
        )
        for n, part in enumerate(parts):
            blend = m[:, n * half : (n + 1) * half] + bias_ref[layer]
            if tile == 16:
                out_ref[:, part] = blend.astype(jnp.bfloat16).reshape(cells, tile, half)
            else:
                out_ref[:, part] = blend.reshape(cells, tile, half).astype(jnp.bfloat16)


def grid_mixing(layer, got, mix, bias):
    return pl.pallas_call(
        functools.partial(grid_kernel, layer),
        out_shape=jax.ShapeDtypeStruct(got.shape, jnp.bfloat16),
        in_specs=[VMEM] * 3,
        out_specs=VMEM,
        compiler_params=pltpu.CompilerParams(vmem_limit_bytes=10 * MIB),
        name="grid_mixing",
    )(got, mix, bias)


def keep_rows(top, bottom, near_ref, far_ref):
    odd_row = parity("row")

    @pl.when(odd_row == 0)
    def _():
        near_ref[...] = bottom
        far_ref[...] = top

    @pl.when(odd_row == 1)
    def _():
        near_ref[...] = top
        far_ref[...] = bottom


def keep_columns(strip_ref, left_ref, right_ref):
    left_ref[...] = strip_ref[0].astype(jnp.bfloat16)
    right_ref[...] = strip_ref[1].astype(jnp.bfloat16)


def back_kernel(layer, last, mixed_ref, gl_ref, gu_ref, gm_ref, proj_ref, *refs):
    if last:
        out_hbm, *refs = refs
        cur_ref = refs[0]
    else:
        cur_ref, *refs = refs
    rows, cols, channels = cur_ref.shape
    many = largest_divisor(rows, 8)

    @pl.loop(0, rows // many)
    def _(g):
        where = pl.ds(pl.multiple_of(g * many * cols, many * cols), many * cols)
        gated = gu_ref[where].astype(jnp.float32) * gm_ref[where].astype(jnp.float32)
        joined = jnp.concatenate([gl_ref[where], gated.astype(jnp.bfloat16)], axis=1)
        total = mixed_ref[where] + jnp.dot(
            joined, proj_ref[layer], preferred_element_type=jnp.float32
        )
        cur_ref[pl.ds(g * many, many)] = total.reshape(many, cols, channels).astype(jnp.bfloat16)
        if last:
            part = pl.ds(g * many, many)
            pltpu.make_async_copy(cur_ref.at[part], out_hbm.at[part], refs[1].at[0]).start()
        else:
            strip_ref = refs[-1]
            for u in range(many):
                for c in range(RIM):
                    low = u * cols + c
                    high = (u + 1) * cols - RIM + c
                    strip_ref[0, c, pl.ds(g * many + u, 1)] = total[low : low + 1]
                    strip_ref[1, c, pl.ds(g * many + u, 1)] = total[high : high + 1]

    if last:
        pltpu.make_async_copy(cur_ref, out_hbm, refs[1].at[0]).wait()
    else:
        *strip_refs, strip_ref = refs
        keep_rows(cur_ref[0:RIM], cur_ref[rows - RIM : rows], *strip_refs[:2])
        keep_columns(strip_ref, *strip_refs[2:])


def strip_shapes(shape):
    rows, cols, channels = shape
    return [jax.ShapeDtypeStruct((RIM, cols, channels), jnp.bfloat16)] * 2 + [
        jax.ShapeDtypeStruct((RIM, rows, channels), jnp.bfloat16)
    ] * 2


def back(layer, last, mixed, gl, gu, gm, proj, shape):
    rows, cols, channels = shape
    f32 = jnp.float32
    outs = [jax.ShapeDtypeStruct(shape, jnp.bfloat16)]
    if last:
        scratch = [pltpu.VMEM(shape, jnp.bfloat16), pltpu.SemaphoreType.DMA((1,))]
    else:
        outs += strip_shapes(shape)
        scratch = [pltpu.VMEM((2, RIM, rows, channels), f32)]
    return pl.pallas_call(
        functools.partial(back_kernel, layer, last),
        out_shape=outs,
        in_specs=[VMEM] * 5,
        out_specs=[ANY] if last else [VMEM] * len(outs),
        scratch_shapes=scratch,
        compiler_params=pltpu.CompilerParams(vmem_limit_bytes=16 * MIB),
        cost_estimate=pl.CostEstimate(
            flops=2 * rows * cols * channels * channels,
            bytes_accessed=rows * cols * channels * 9,
            transcendentals=0,
        ),
        name="back",
    )(mixed, gl, gu, gm, proj)


def row_strips_kernel(image_hbm, near_ref, far_ref, edge_ref, sems):
    rows = image_hbm.shape[0]
    copies = [
        pltpu.make_async_copy(image_hbm.at[0:RIM], edge_ref.at[0], sems.at[0]),
        pltpu.make_async_copy(image_hbm.at[rows - RIM : rows], edge_ref.at[1], sems.at[1]),
    ]
    for copy in copies:
        copy.start()
    for copy in copies:
        copy.wait()
    keep_rows(edge_ref[0], edge_ref[1], near_ref, far_ref)


def row_strips(image):
    _, cols, channels = image.shape
    return pl.pallas_call(
        row_strips_kernel,
        out_shape=strip_shapes(image.shape)[:2],
        in_specs=[ANY],
        out_specs=[VMEM] * 2,
        scratch_shapes=[
            pltpu.VMEM((2, RIM, cols, channels), jnp.bfloat16),
            pltpu.SemaphoreType.DMA((2,)),
        ],
        compiler_params=pltpu.CompilerParams(vmem_limit_bytes=8 * MIB),
        name="row_strips",
    )(in_hbm(image))


def column_strips_kernel(image_hbm, cur_ref, left_ref, right_ref, strip_ref, sem):
    rows, cols, _ = image_hbm.shape
    copy = pltpu.make_async_copy(image_hbm, cur_ref, sem.at[0])
    copy.start()
    copy.wait()
    side = math.gcd(cols, 16)
    for i in range(rows):
        low = cur_ref[i, 0:side].astype(jnp.float32)
        high = cur_ref[i, cols - side : cols].astype(jnp.float32)
        for c in range(RIM):
            strip_ref[0, c, i : i + 1] = low[c : c + 1]
            strip_ref[1, c, i : i + 1] = high[side - RIM + c : side - RIM + c + 1]
    keep_columns(strip_ref, left_ref, right_ref)


def column_strips(image):
    rows, _, channels = image.shape
    return pl.pallas_call(
        column_strips_kernel,
        out_shape=[jax.ShapeDtypeStruct(image.shape, jnp.bfloat16)]
        + strip_shapes(image.shape)[2:],
        in_specs=[ANY],
        out_specs=[VMEM] * 3,
        scratch_shapes=[
            pltpu.VMEM((2, RIM, rows, channels), jnp.float32),
            pltpu.SemaphoreType.DMA((1,)),
        ],
        compiler_params=pltpu.CompilerParams(vmem_limit_bytes=8 * MIB),
        cost_estimate=pl.CostEstimate(flops=0, bytes_accessed=8 * MIB, transcendentals=0),
        name="column_strips",
    )(in_hbm(image))


def traded(axis, near, far, around):
    count = lax.axis_size(axis)
    inner = [(i, i ^ 1) for i in range(count)]
    outer = [(i, (i + 1) % count) for i in range(1, count if around else count - 1, 2)]
    outer += [(target, source) for source, target in outer]
    far = lax.ppermute(far, axis, outer)
    near = lax.ppermute(near, axis, inner)
    return near, far


def columns_kernel(near_rows, far_rows, left_ref, right_ref, near_ref, far_ref):
    odd_row, odd_col = parity("row"), parity("col")
    rim, _, _ = left_ref.shape
    cols = near_rows.shape[1]
    near_top = odd_row == 1
    for side, own_ref in ((0, left_ref), (1, right_ref)):
        wanted = (odd_col == 1) if side == 0 else (odd_col == 0)
        first = 0 if side == 0 else cols - rim

        def ends(rows_ref, c):
            return [rows_ref[r, first + c : first + c + 1].astype(jnp.float32) for r in range(rim)]

        strips = []
        for c in range(rim):
            close, other = ends(near_rows, c), ends(far_rows, c)
            top = [jnp.where(near_top, x, y) for x, y in zip(close, other)]
            bottom = [jnp.where(near_top, y, x) for x, y in zip(close, other)]
            strips.append(
                jnp.concatenate(top + [own_ref[c].astype(jnp.float32)] + bottom, axis=0).astype(
                    jnp.bfloat16
                )
            )

        @pl.when(wanted)
        def _():
            for c in range(rim):
                near_ref[c] = strips[c]

        @pl.when(jnp.logical_not(wanted))
        def _():
            for c in range(rim):
                far_ref[c] = strips[c]


def columns(near_rows, far_rows, left, right):
    rim, rows, channels = left.shape
    return pl.pallas_call(
        columns_kernel,
        out_shape=[jax.ShapeDtypeStruct((rim, rows + 2 * rim, channels), jnp.bfloat16)] * 2,
        in_specs=[VMEM] * 4,
        out_specs=[VMEM] * 2,
        compiler_params=pltpu.CompilerParams(vmem_limit_bytes=8 * MIB),
        name="columns",
    )(near_rows, far_rows, left, right)


def rims(near_rows, far_rows, left, right):
    rim_rows = traded("row", near_rows, far_rows, True)
    return rim_rows, traded("col", *columns(*rim_rows, left, right), False)


def on_device(
    image,
    norm_gain,
    conv_first,
    conv_second,
    proj_in,
    block_mix,
    block_bias,
    grid_mix,
    grid_bias,
    proj_out,
):
    rows, cols, channels = image.shape
    half = channels // 2
    row_count = lax.axis_size("row")
    col_count = lax.axis_size("col")
    cells = row_count * col_count
    pixels = rows * cols
    share = pixels // cells
    tile = math.gcd(share, 16)
    first = conv_first.reshape(LAYERS, 9 * channels, channels)
    second = conv_second.reshape(LAYERS, 9 * channels, channels)
    near_rows, far_rows = row_strips(image)
    current, left, right = column_strips(image)
    mix_tiles, bias_tiles = mixing_tiles(grid_mix, grid_bias, tile, half)
    own = (near_rows, far_rows, left, right)
    for layer in range(LAYERS):
        last = layer == LAYERS - 1
        rim_rows, rim_cols = rims(*own)
        mixed, lu, lv, gu, gv = front(
            layer, current, rim_rows, rim_cols, norm_gain, first, second, proj_in
        )
        gl = local(
            layer,
            lu.reshape(rows, cols, half),
            lv.reshape(rows, cols, half),
            block_mix,
            block_bias,
        )
        gv, gl = lax.optimization_barrier((gv, gl))
        got = lax.all_to_all(gv.reshape(1, cells, share, half), ("row", "col"), 1, 0, tiled=True)
        blend = grid_mixing(layer, got.reshape(cells, share, half), mix_tiles, bias_tiles)
        gm = lax.all_to_all(blend.reshape(cells, 1, share, half), ("row", "col"), 0, 1, tiled=True)
        current, *own = back(
            layer,
            last,
            mixed,
            gl.reshape(pixels, half),
            gu,
            gm.reshape(pixels, half),
            proj_out,
            image.shape,
        )
    return current


def solution(mesh):
    placed = (P("row", "col", None), P(), P(), P(), P(), P(), P(), P(), P(), P())
    return jax.shard_map(
        on_device, mesh=mesh, in_specs=placed, out_specs=P("row", "col", None), check_vma=False
    )
```

```python
import functools
import math

import jax
import jax.numpy as jnp
from jax import lax
from jax.experimental import pallas as pl
from jax.experimental.pallas import tpu as pltpu
from jax.sharding import PartitionSpec as P


BLOCK = 16
LAYERS = 2
RIM = 2
GROUP_ONE = 5
GROUP_TWO = 12
MIB = 1 << 20

epsilon = 1e-06
ROOT = math.sqrt(2.0 / math.pi)

VMEM = pl.BlockSpec(memory_space=pltpu.VMEM)
ANY = pl.BlockSpec(memory_space=pltpu.HBM)


def parity(axis):
    return lax.rem(lax.axis_index(axis), 2)


def edge_factors():
    factors = []
    for axis in ("row", "col"):
        place = lax.axis_index(axis)
        for end in (0, lax.axis_size(axis) - 1):
            factors.append(jnp.where(place == end, 0.0, 1.0))
    return factors


def gelu(v):
    return 0.5 * v * (1.0 + jnp.tanh(ROOT * (v + 0.044715 * (v * v * v))))


def normalised(values, gain_row):
    average = jnp.mean(values, axis=-1, keepdims=True)
    centred = values - average
    variance = jnp.mean(centred * centred, axis=-1, keepdims=True)
    return centred * lax.rsqrt(variance + epsilon) * gain_row


def rounded(values):
    return values.astype(jnp.bfloat16).astype(jnp.float32)


def largest_divisor(total, most):
    return max(d for d in range(1, most + 1) if total % d == 0)


def spread(row, left_row, right_row, dst_ref, i, cols):
    channels = row.shape[-1]
    place = lax.broadcasted_iota(jnp.int32, row.shape, 0)
    before = jnp.where(place == 0, left_row, pltpu.roll(row, 1, 0))
    after = jnp.where(place == cols - 1, right_row, pltpu.roll(row, cols - 1, 0))
    dst_ref[i, :, 0:channels] = before.astype(jnp.bfloat16)
    dst_ref[i, :, channels : 2 * channels] = row.astype(jnp.bfloat16)
    dst_ref[i, :, 2 * channels : 3 * channels] = after.astype(jnp.bfloat16)


def in_hbm(values):
    return pltpu.with_memory_space_constraint(values, pltpu.HBM)


def front_kernel(
    layer,
    cur_ref,
    near_rows,
    far_rows,
    near_cols,
    far_cols,
    gain_hbm,
    first_hbm,
    second_hbm,
    in_proj_hbm,
    mixed_ref,
    lu_ref,
    lv_ref,
    gu_ref,
    gv_ref,
    one_ref,
    two_ref,
    sides_ref,
    left_side,
    right_side,
    left_one,
    right_one,
    slot_a,
    slot_b,
    slot_c,
    slot_d,
    first_ref,
    second_ref,
    in_ref,
    gain_ref,
    sems,
):
    rows, cols, channels = cur_ref.shape
    feed = [
        pltpu.make_async_copy(src.at[layer], dst, sems.at[k])
        for k, (src, dst) in enumerate(
            ((first_hbm, first_ref), (second_hbm, second_ref), (in_proj_hbm, in_ref))
        )
    ]
    gain_copy = pltpu.make_async_copy(gain_hbm.at[layer], gain_ref, sems.at[3])
    gain_copy.start()
    for copy in feed:
        copy.start()
    half = channels // 2
    near_top = parity("row") == 1
    near_left = parity("col") == 1
    edge_ref = edge_factors()
    gain_copy.wait()
    gain_one = gain_ref[0:1, :]
    gain_two = gain_ref[1:2, :]
    long = rows + 2 * RIM

    spot = lax.broadcasted_iota(jnp.int32, (long, channels), 0)
    within = jnp.where(spot < RIM, edge_ref[0], jnp.where(spot < long - RIM, 1.0, edge_ref[1]))

    def chosen(near_low, side, near, far):
        low, high = (near, far) if side == 0 else (far, near)
        return jnp.where(near_low, low.astype(jnp.float32), high.astype(jnp.float32))

    for side in range(2):
        for c in range(RIM):
            sides_ref[side * RIM + c, 0:long] = rounded(
                normalised(chosen(near_left, side, near_cols[c], far_cols[c]), gain_one)
            ) * (within * edge_ref[2 + side])
    left_side[0:long, 0:channels] = sides_ref[0, 0:long]
    left_side[0:long, channels : 2 * channels] = sides_ref[1, 0:long]
    right_side[0:long, channels : 2 * channels] = sides_ref[2, 0:long]
    right_side[0:long, 2 * channels : 3 * channels] = sides_ref[3, 0:long]

    def norm_row(values, dst, keep=None):
        row = rounded(normalised(values, gain_one))
        if keep is not None:
            row = row * keep
        spread(row, sides_ref[1, dst : dst + 1], sides_ref[2, dst : dst + 1], one_ref, dst, cols)
        left_side[dst : dst + 1, 2 * channels : 3 * channels] = row[0:1]
        right_side[dst : dst + 1, 0:channels] = row[cols - 1 : cols]

    def norm_any(dst):
        if dst < RIM:
            norm_row(chosen(near_top, 0, near_rows[dst], far_rows[dst]), dst, edge_ref[0])
        elif dst < RIM + rows:
            norm_row(cur_ref[dst - RIM].astype(jnp.float32), dst)
        else:
            r = dst - RIM - rows
            norm_row(chosen(near_top, 1, near_rows[r], far_rows[r]), dst, edge_ref[1])

    def windows(src_ref, base, count):
        return jnp.concatenate(
            [
                src_ref[pl.ds(base + a, count)].reshape(count * cols, 3 * channels)
                for a in range(3)
            ],
            axis=1,
        )

    tall = rows + 2
    group = slot_a.shape[0] // cols
    first_steps = tall // group
    ends = -(-group // 16) * 16

    def first_multiply(g, slot):
        base = g * group
        sides = [
            jnp.concatenate([side[base + a : base + a + ends] for a in range(3)], axis=1)
            for side in (left_side, right_side)
        ]
        window = jnp.concatenate(
            [windows(one_ref, base, group)] + [v.astype(jnp.bfloat16) for v in sides], axis=0
        )
        total = jnp.dot(window, first_ref[...], preferred_element_type=jnp.float32)
        slot[...] = total[: group * cols]
        place = lax.broadcasted_iota(jnp.int32, (ends, channels), 0) + base
        inside = jnp.where(place == 0, edge_ref[0], jnp.where(place == tall - 1, edge_ref[1], 1.0))
        for k, one_side in enumerate((left_one, right_one)):
            start = group * cols + k * ends
            part = rounded(gelu(total[start : start + ends]) * (inside * edge_ref[2 + k]))
            one_side[base : base + group] = part[:group]

    def first_finish(g, slot):
        for u in range(group):
            i = g * group + u
            row = rounded(gelu(slot[u * cols : (u + 1) * cols]))
            if i == 0:
                row = row * edge_ref[0]
            if i == tall - 1:
                row = row * edge_ref[1]
            spread(row, left_one[i : i + 1], right_one[i : i + 1], two_ref, i, cols)

    many = slot_c.shape[0] // cols

    def second_multiply(g, slot):
        slot[...] = jnp.dot(
            windows(two_ref, g * many, many),
            second_ref[...],
            preferred_element_type=jnp.float32,
        )

    def second_finish(g, slot):
        where = slice(g * many * cols, (g + 1) * many * cols)
        total = slot[...] + cur_ref[pl.ds(g * many, many)].reshape(
            many * cols, channels
        ).astype(jnp.float32)
        mixed_ref[where] = total
        normed = normalised(total, gain_two).astype(jnp.bfloat16)
        expanded = gelu(
            jnp.dot(normed, in_ref[...], preferred_element_type=jnp.float32)
        ).astype(jnp.bfloat16)
        for k, out in enumerate((lu_ref, lv_ref, gu_ref, gv_ref)):
            out[where] = expanded[:, k * half : (k + 1) * half]

    second_steps = rows // many
    slots = (slot_a, slot_b)
    others = (slot_c, slot_d)

    def norm_group(g):
        begin = 0 if g == 0 else g * group + 2
        for dst in range(begin, (g + 1) * group + 2):
            norm_any(dst)

    norm_group(0)
    feed[0].wait()
    for g in range(first_steps):
        first_multiply(g, slots[g % 2])
        if g > 0:
            first_finish(g - 1, slots[(g - 1) % 2])
        if g + 1 < first_steps:
            norm_group(g + 1)
    feed[1].wait()
    feed[2].wait()
    second_multiply(0, others[0])
    first_finish(first_steps - 1, slots[(first_steps - 1) % 2])
    for g in range(1, second_steps):
        second_multiply(g, others[g % 2])
        second_finish(g - 1, others[(g - 1) % 2])
    second_finish(second_steps - 1, others[(second_steps - 1) % 2])


def front(layer, cur, rim_rows, rim_cols, gains, first, second, proj):
    rows, cols, channels = cur.shape
    pixels = rows * cols
    half = channels // 2
    long = rows + 2 * RIM
    tall = -(-(rows + 2) // 16) * 16 + 16
    group = largest_divisor(rows + 2, GROUP_ONE)
    many = largest_divisor(rows, GROUP_TWO)
    bf = jnp.bfloat16
    f32 = jnp.float32
    outs = [jax.ShapeDtypeStruct((pixels, channels), f32)]
    outs += [jax.ShapeDtypeStruct((pixels, half), bf)] * 4
    return pl.pallas_call(
        functools.partial(front_kernel, layer),
        out_shape=outs,
        in_specs=[VMEM] * 5 + [ANY] * 4,
        out_specs=[VMEM] * 5,
        scratch_shapes=[
            pltpu.VMEM((long, cols, 3 * channels), bf),
            pltpu.VMEM((rows + 2, cols, 3 * channels), bf),
            pltpu.VMEM((2 * RIM, tall, channels), f32),
            pltpu.VMEM((tall, 3 * channels), f32),
            pltpu.VMEM((tall, 3 * channels), f32),
            pltpu.VMEM((rows + 2, channels), f32),
            pltpu.VMEM((rows + 2, channels), f32),
            pltpu.VMEM((group * cols, channels), f32),
            pltpu.VMEM((group * cols, channels), f32),
            pltpu.VMEM((many * cols, channels), f32),
            pltpu.VMEM((many * cols, channels), f32),
            pltpu.VMEM(first.shape[1:], bf),
            pltpu.VMEM(second.shape[1:], bf),
            pltpu.VMEM(proj.shape[1:], bf),
            pltpu.VMEM(gains.shape[1:], f32),
            pltpu.SemaphoreType.DMA((4,)),
        ],
        compiler_params=pltpu.CompilerParams(vmem_limit_bytes=34 * MIB),
        cost_estimate=pl.CostEstimate(
            flops=2 * pixels * channels * channels * 20,
            bytes_accessed=12 << 20,
            transcendentals=3 * pixels * channels,
        ),
        name="front",
    )(cur, *rim_rows, *rim_cols, *(in_hbm(w) for w in (gains, first, second, proj)))


def local_kernel(layer, lu_ref, lv_ref, mix_ref, bias_ref, out_ref):
    rows, cols, half = lu_ref.shape
    down, across = rows // BLOCK, cols // BLOCK
    pair = 2 if across % 2 == 0 else 1
    area = BLOCK * BLOCK
    spot = lax.broadcasted_iota(jnp.int32, (area, area), 0)
    same = spot == lax.broadcasted_iota(jnp.int32, (area, area), 1)
    bias = jnp.sum(jnp.where(same, bias_ref[layer : layer + 1], 0.0), axis=1, keepdims=True)
    for i in range(down):
        r = slice(i * BLOCK, (i + 1) * BLOCK)
        for j in range(0, across, pair):
            cut = [slice((j + k) * BLOCK, (j + k + 1) * BLOCK) for k in range(pair)]
            v = jnp.concatenate(
                [lv_ref[r, c].reshape(BLOCK * BLOCK, half) for c in cut], axis=1
            )
            m = jnp.dot(mix_ref[layer], v, preferred_element_type=jnp.float32) + bias
            for k, c in enumerate(cut):
                u = lu_ref[r, c].reshape(BLOCK * BLOCK, half).astype(jnp.float32)
                gated = (u * m[:, k * half : (k + 1) * half]).astype(jnp.bfloat16)
                out_ref[r, c] = gated.reshape(BLOCK, BLOCK, half)


def tiles_kernel(grid_ref, grid_bias_ref, tiles_ref, shift_ref):
    cells = grid_ref.shape[-1]
    wide = tiles_ref.shape[1]
    tile = wide // cells
    down_of = lax.broadcasted_iota(jnp.int32, (wide, cells), 0) // tile
    chosen = down_of == lax.broadcasted_iota(jnp.int32, (wide, cells), 1)
    for layer in range(grid_ref.shape[0]):
        shift = jnp.sum(jnp.where(chosen, grid_bias_ref[layer : layer + 1], 0.0), axis=1, keepdims=True)
        shift_ref[layer] = jnp.broadcast_to(shift, shift_ref.shape[1:])
        pick = chosen.astype(jnp.bfloat16)
        across_of = lax.broadcasted_iota(jnp.int32, (cells, wide), 1) // tile
        lay = (across_of == lax.broadcasted_iota(jnp.int32, (cells, wide), 0)).astype(jnp.bfloat16)
        tall = jnp.dot(pick, grid_ref[layer], preferred_element_type=jnp.float32)
        full = jnp.dot(tall.astype(jnp.bfloat16), lay, preferred_element_type=jnp.float32)
        p = lax.broadcasted_iota(jnp.int32, (wide, wide), 0) % tile
        q = lax.broadcasted_iota(jnp.int32, (wide, wide), 1) % tile
        tiles_ref[layer] = jnp.where(p == q, full, 0.0).astype(jnp.bfloat16)


def mixing_tiles(grid, grid_bias, tile, half):
    layers, cells, _ = grid.shape
    wide = cells * tile
    return pl.pallas_call(
        tiles_kernel,
        out_shape=[
            jax.ShapeDtypeStruct((layers, wide, wide), jnp.bfloat16),
            jax.ShapeDtypeStruct((layers, wide, half), jnp.float32),
        ],
        in_specs=[VMEM] * 2,
        out_specs=[VMEM] * 2,
        compiler_params=pltpu.CompilerParams(vmem_limit_bytes=24 * MIB),
        cost_estimate=pl.CostEstimate(flops=0, bytes_accessed=4 * MIB, transcendentals=0),
        name="mixing_tiles",
    )(grid, grid_bias)


def local(layer, lu, lv, mix, bias):
    rows, cols, half = lu.shape
    return pl.pallas_call(
        functools.partial(local_kernel, layer),
        out_shape=jax.ShapeDtypeStruct(lu.shape, jnp.bfloat16),
        in_specs=[VMEM] * 4,
        out_specs=VMEM,
        compiler_params=pltpu.CompilerParams(vmem_limit_bytes=12 * MIB),
        cost_estimate=pl.CostEstimate(
            flops=2 * rows * cols * half * BLOCK * BLOCK,
            bytes_accessed=6 * rows * cols * half,
            transcendentals=0,
        ),
        name="local",
    )(lu, lv, mix, bias)


def grid_kernel(layer, got_ref, mix_ref, bias_ref, out_ref):
    cells, share, half = got_ref.shape
    tile = mix_ref.shape[1] // cells
    step = 2 * tile if share % (2 * tile) == 0 else tile
    for k in range(share // step):
        parts = [slice(t, t + tile) for t in range(k * step, (k + 1) * step, tile)]
        if tile == 16:
            v = [got_ref[:, part].reshape(cells * tile, half) for part in parts]
        else:
            v = [
                got_ref[:, part].astype(jnp.float32).reshape(cells * tile, half).astype(jnp.bfloat16)
                for part in parts
            ]
        m = jnp.dot(
            mix_ref[layer], jnp.concatenate(v, axis=1), preferred_element_type=jnp.float32
        )
        for n, part in enumerate(parts):
            blend = m[:, n * half : (n + 1) * half] + bias_ref[layer]
            if tile == 16:
                out_ref[:, part] = blend.astype(jnp.bfloat16).reshape(cells, tile, half)
            else:
                out_ref[:, part] = blend.reshape(cells, tile, half).astype(jnp.bfloat16)


def grid_mixing(layer, got, mix, bias):
    return pl.pallas_call(
        functools.partial(grid_kernel, layer),
        out_shape=jax.ShapeDtypeStruct(got.shape, jnp.bfloat16),
        in_specs=[VMEM] * 3,
        out_specs=VMEM,
        compiler_params=pltpu.CompilerParams(vmem_limit_bytes=10 * MIB),
        name="grid_mixing",
    )(got, mix, bias)


def keep_rows(top, bottom, near_ref, far_ref):
    odd_row = parity("row")

    @pl.when(odd_row == 0)
    def _():
        near_ref[...] = bottom
        far_ref[...] = top

    @pl.when(odd_row == 1)
    def _():
        near_ref[...] = top
        far_ref[...] = bottom


def keep_columns(strip_ref, left_ref, right_ref):
    left_ref[...] = strip_ref[0].astype(jnp.bfloat16)
    right_ref[...] = strip_ref[1].astype(jnp.bfloat16)


def back_kernel(layer, last, mixed_ref, gl_ref, gu_ref, gm_ref, proj_ref, *refs):
    if last:
        out_hbm, *refs = refs
        cur_ref = refs[0]
    else:
        cur_ref, *refs = refs
    rows, cols, channels = cur_ref.shape
    many = largest_divisor(rows, 8)

    @pl.loop(0, rows // many)
    def _(g):
        where = pl.ds(pl.multiple_of(g * many * cols, many * cols), many * cols)
        gated = gu_ref[where].astype(jnp.float32) * gm_ref[where].astype(jnp.float32)
        joined = jnp.concatenate([gl_ref[where], gated.astype(jnp.bfloat16)], axis=1)
        total = mixed_ref[where] + jnp.dot(
            joined, proj_ref[layer], preferred_element_type=jnp.float32
        )
        cur_ref[pl.ds(g * many, many)] = total.reshape(many, cols, channels).astype(jnp.bfloat16)
        if last:
            part = pl.ds(g * many, many)
            pltpu.make_async_copy(cur_ref.at[part], out_hbm.at[part], refs[1].at[0]).start()
        else:
            strip_ref = refs[-1]
            for u in range(many):
                for c in range(RIM):
                    low = u * cols + c
                    high = (u + 1) * cols - RIM + c
                    strip_ref[0, c, pl.ds(g * many + u, 1)] = total[low : low + 1]
                    strip_ref[1, c, pl.ds(g * many + u, 1)] = total[high : high + 1]

    if last:
        pltpu.make_async_copy(cur_ref, out_hbm, refs[1].at[0]).wait()
    else:
        *strip_refs, strip_ref = refs
        keep_columns(strip_ref, *strip_refs)


def ends_kernel(layer, mixed_ref, gl_ref, gu_ref, gm_ref, proj_ref, near_ref, far_ref):
    pixels = mixed_ref.shape[0]
    wide = near_ref.shape[0] * near_ref.shape[1]
    found = []
    for where in (slice(0, wide), slice(pixels - wide, pixels)):
        gated = gu_ref[where].astype(jnp.float32) * gm_ref[where].astype(jnp.float32)
        joined = jnp.concatenate([gl_ref[where], gated.astype(jnp.bfloat16)], axis=1)
        total = mixed_ref[where] + jnp.dot(
            joined, proj_ref[layer], preferred_element_type=jnp.float32
        )
        found.append(total.reshape(near_ref.shape).astype(jnp.bfloat16))
    keep_rows(*found, near_ref, far_ref)


def row_ends(layer, mixed, gl, gu, gm, proj, shape):
    return pl.pallas_call(
        functools.partial(ends_kernel, layer),
        out_shape=strip_shapes(shape)[:2],
        in_specs=[VMEM] * 5,
        out_specs=[VMEM] * 2,
        compiler_params=pltpu.CompilerParams(vmem_limit_bytes=16 * MIB),
        name="row_ends",
    )(mixed, gl, gu, gm, proj)


def strip_shapes(shape):
    rows, cols, channels = shape
    return [jax.ShapeDtypeStruct((RIM, cols, channels), jnp.bfloat16)] * 2 + [
        jax.ShapeDtypeStruct((RIM, rows, channels), jnp.bfloat16)
    ] * 2


def back(layer, last, mixed, gl, gu, gm, proj, shape):
    rows, cols, channels = shape
    f32 = jnp.float32
    outs = [jax.ShapeDtypeStruct(shape, jnp.bfloat16)]
    if last:
        scratch = [pltpu.VMEM(shape, jnp.bfloat16), pltpu.SemaphoreType.DMA((1,))]
    else:
        outs += strip_shapes(shape)[2:]
        scratch = [pltpu.VMEM((2, RIM, rows, channels), f32)]
    return pl.pallas_call(
        functools.partial(back_kernel, layer, last),
        out_shape=outs,
        in_specs=[VMEM] * 5,
        out_specs=[ANY] if last else [VMEM] * len(outs),
        scratch_shapes=scratch,
        compiler_params=pltpu.CompilerParams(vmem_limit_bytes=16 * MIB),
        cost_estimate=pl.CostEstimate(
            flops=2 * rows * cols * channels * channels,
            bytes_accessed=rows * cols * channels * 9,
            transcendentals=0,
        ),
        name="back",
    )(mixed, gl, gu, gm, proj)


def row_strips_kernel(image_hbm, near_ref, far_ref, edge_ref, sems):
    rows = image_hbm.shape[0]
    copies = [
        pltpu.make_async_copy(image_hbm.at[0:RIM], edge_ref.at[0], sems.at[0]),
        pltpu.make_async_copy(image_hbm.at[rows - RIM : rows], edge_ref.at[1], sems.at[1]),
    ]
    for copy in copies:
        copy.start()
    for copy in copies:
        copy.wait()
    keep_rows(edge_ref[0], edge_ref[1], near_ref, far_ref)


def row_strips(image):
    _, cols, channels = image.shape
    return pl.pallas_call(
        row_strips_kernel,
        out_shape=strip_shapes(image.shape)[:2],
        in_specs=[ANY],
        out_specs=[VMEM] * 2,
        scratch_shapes=[
            pltpu.VMEM((2, RIM, cols, channels), jnp.bfloat16),
            pltpu.SemaphoreType.DMA((2,)),
        ],
        compiler_params=pltpu.CompilerParams(vmem_limit_bytes=8 * MIB),
        name="row_strips",
    )(in_hbm(image))


def column_strips_kernel(image_hbm, cur_ref, left_ref, right_ref, strip_ref, sem):
    rows, cols, _ = image_hbm.shape
    copy = pltpu.make_async_copy(image_hbm, cur_ref, sem.at[0])
    copy.start()
    copy.wait()
    side = math.gcd(cols, 16)
    for i in range(rows):
        low = cur_ref[i, 0:side].astype(jnp.float32)
        high = cur_ref[i, cols - side : cols].astype(jnp.float32)
        for c in range(RIM):
            strip_ref[0, c, i : i + 1] = low[c : c + 1]
            strip_ref[1, c, i : i + 1] = high[side - RIM + c : side - RIM + c + 1]
    keep_columns(strip_ref, left_ref, right_ref)


def column_strips(image):
    rows, _, channels = image.shape
    return pl.pallas_call(
        column_strips_kernel,
        out_shape=[jax.ShapeDtypeStruct(image.shape, jnp.bfloat16)]
        + strip_shapes(image.shape)[2:],
        in_specs=[ANY],
        out_specs=[VMEM] * 3,
        scratch_shapes=[
            pltpu.VMEM((2, RIM, rows, channels), jnp.float32),
            pltpu.SemaphoreType.DMA((1,)),
        ],
        compiler_params=pltpu.CompilerParams(vmem_limit_bytes=8 * MIB),
        cost_estimate=pl.CostEstimate(flops=0, bytes_accessed=8 * MIB, transcendentals=0),
        name="column_strips",
    )(in_hbm(image))


def traded(axis, near, far, around):
    count = lax.axis_size(axis)
    inner = [(i, i ^ 1) for i in range(count)]
    outer = [(i, (i + 1) % count) for i in range(1, count if around else count - 1, 2)]
    outer += [(target, source) for source, target in outer]
    far = lax.ppermute(far, axis, outer)
    near = lax.ppermute(near, axis, inner)
    return near, far


def columns_kernel(near_rows, far_rows, left_ref, right_ref, near_ref, far_ref):
    odd_row, odd_col = parity("row"), parity("col")
    rim, _, _ = left_ref.shape
    cols = near_rows.shape[1]
    near_top = odd_row == 1
    for side, own_ref in ((0, left_ref), (1, right_ref)):
        wanted = (odd_col == 1) if side == 0 else (odd_col == 0)
        first = 0 if side == 0 else cols - rim

        def ends(rows_ref, c):
            return [rows_ref[r, first + c : first + c + 1].astype(jnp.float32) for r in range(rim)]

        strips = []
        for c in range(rim):
            close, other = ends(near_rows, c), ends(far_rows, c)
            top = [jnp.where(near_top, x, y) for x, y in zip(close, other)]
            bottom = [jnp.where(near_top, y, x) for x, y in zip(close, other)]
            strips.append(
                jnp.concatenate(top + [own_ref[c].astype(jnp.float32)] + bottom, axis=0).astype(
                    jnp.bfloat16
                )
            )

        @pl.when(wanted)
        def _():
            for c in range(rim):
                near_ref[c] = strips[c]

        @pl.when(jnp.logical_not(wanted))
        def _():
            for c in range(rim):
                far_ref[c] = strips[c]


def columns(near_rows, far_rows, left, right):
    rim, rows, channels = left.shape
    return pl.pallas_call(
        columns_kernel,
        out_shape=[jax.ShapeDtypeStruct((rim, rows + 2 * rim, channels), jnp.bfloat16)] * 2,
        in_specs=[VMEM] * 4,
        out_specs=[VMEM] * 2,
        compiler_params=pltpu.CompilerParams(vmem_limit_bytes=8 * MIB),
        name="columns",
    )(near_rows, far_rows, left, right)


def rims(near_rows, far_rows, left, right):
    rim_rows = traded("row", near_rows, far_rows, True)
    return rim_rows, traded("col", *columns(*rim_rows, left, right), False)


def on_device(
    image,
    norm_gain,
    conv_first,
    conv_second,
    proj_in,
    block_mix,
    block_bias,
    grid_mix,
    grid_bias,
    proj_out,
):
    rows, cols, channels = image.shape
    half = channels // 2
    row_count = lax.axis_size("row")
    col_count = lax.axis_size("col")
    cells = row_count * col_count
    pixels = rows * cols
    share = pixels // cells
    tile = math.gcd(share, 16)
    first = conv_first.reshape(LAYERS, 9 * channels, channels)
    second = conv_second.reshape(LAYERS, 9 * channels, channels)
    near_rows, far_rows = row_strips(image)
    current, left, right = column_strips(image)
    mix_tiles, bias_tiles = mixing_tiles(grid_mix, grid_bias, tile, half)
    own = (near_rows, far_rows, left, right)
    for layer in range(LAYERS):
        last = layer == LAYERS - 1
        rim_rows, rim_cols = rims(*own)
        mixed, lu, lv, gu, gv = front(
            layer, current, rim_rows, rim_cols, norm_gain, first, second, proj_in
        )
        gl = local(
            layer,
            lu.reshape(rows, cols, half),
            lv.reshape(rows, cols, half),
            block_mix,
            block_bias,
        )
        gv, gl = lax.optimization_barrier((gv, gl))
        got = lax.all_to_all(gv.reshape(1, cells, share, half), ("row", "col"), 1, 0, tiled=True)
        blend = grid_mixing(layer, got.reshape(cells, share, half), mix_tiles, bias_tiles)
        gm = lax.all_to_all(blend.reshape(cells, 1, share, half), ("row", "col"), 0, 1, tiled=True)
        parts = (mixed, gl.reshape(pixels, half), gu, gm.reshape(pixels, half), proj_out)
        if last:
            (current,) = back(layer, last, *parts, image.shape)
        else:
            rows_own = row_ends(layer, *parts, image.shape)
        if not last:
            current, *cols_own = back(layer, last, *parts, image.shape)
            own = (*rows_own, *cols_own)
    return current


def solution(mesh):
    placed = (P("row", "col", None), P(), P(), P(), P(), P(), P(), P(), P(), P())
    return jax.shard_map(
        on_device, mesh=mesh, in_specs=placed, out_specs=P("row", "col", None), check_vma=False
    )
```
